32 devices in a mesh: groups: 2 (over y), expert: 4 (over z), dp: 2 (over x), head: 2 (over core).
Axes of the slice: x: 2, y: 2, z: 4, core: 2. Of those that a mesh axis runs over, the one named last changes fastest.
Arguments:
- hidden: bfloat16 [4, 1024, 1536], P(('groups', 'dp'), ('expert', 'head')), parts along dimension 0, may hold values from -6 to 6
- modulation: float32 [4, 3, 1536], P(('groups', 'dp')), parts along dimension 0, may hold values from -3 to 3
- router_weight: float32 [1536, 16], replicated, may hold values from -0.15625 to 0.15625
- route_ids: int32 [4, 1024, 2], P(('groups', 'dp'), ('expert', 'head')), parts along dimension 0, may hold values from 0 to 15, all different within a row; in each aligned block of 128 rows (0 to 127, 128 to 255, ..., all dimensions but the last counted through in order) at most 32 rows name the same one
- gate_weight: bfloat16 [1536, 98304], P(None, ('expert', 'dp', 'head')), may hold values from -0.15625 to 0.15625
- up_weight: bfloat16 [1536, 98304], P(None, ('expert', 'dp', 'head')), may hold values from -0.15625 to 0.15625
- down_weight: bfloat16 [98304, 1536], P(('expert', 'dp', 'head')), may hold values from -0.078125 to 0.078125
- main_final: bfloat16 [1536, 16], replicated, may hold values from -0.15625 to 0.15625
- guide_qkv: bfloat16 [4, 1024, 6, 192], P(('groups', 'dp'), 'expert', 'head'), parts along dimension 0, may hold values from -6 to 6
- guide_out: bfloat16 [6, 64, 384], P('head'), may hold values from -0.3125 to 0.3125
- guide_final: bfloat16 [384, 16], replicated, may hold values from -0.3125 to 0.3125
- latent: float32 [4, 1024, 16], P(('groups', 'dp'), ('expert', 'head')), parts along dimension 0, may hold values from -6 to 6
- guidance: float32 [4], P(('groups', 'dp')), parts along dimension 0, may hold values from 1.5 to 3
- step_size: float32 [4], P(('groups', 'dp')), parts along dimension 0, may hold values from 0.1 to 0.5
Outputs:
- next_latent: float32 [4, 1024, 16], P(('groups', 'dp'), ('expert', 'head')), parts along dimension 0
The draws below stay inside these ranges and needn't reach their ends.
There are 2 independent parts, one for each index of `groups`. The reference program is written for one: setup_inputs(seed, part) draws one part's arguments, and reference() takes and returns one part's arrays. A program takes and returns all parts, laid end to end along the dimension named above; an argument that names none is the same for every part. Nothing has to cross between parts.
Inputs may be any that keep to these rules, and one draw needn't show every extreme that they name: `route_ids`: each token names 2 different experts. In each aligned block of 128 tokens of a latent (tokens 128 j to 128 (j + 1) - 1), no expert is named by more than 32 routes, a bound that some block reaches.
All inputs are finite; a program needn't handle non-finite values.
Results may differ from the reference program's by a relative error of at most 0.0065.
Values may be sent and summed in bfloat16 or wider, within the bound.
No kernel may reach another device: no remote copies, remote signals or barrier semaphores. Data moves between devices by JAX's collectives and lax.ppermute only.
A program may use at most 192 MiB of HBM per device.

```python
import math
import jax
import jax.numpy as jnp
import numpy as np
from jax import lax

D = 1536
FF = 6144
EXPERTS = 16
TOP = 2
GH = 6
HD = 64
DG = 384
P_SIZE = 16
SEQ = 1024
LATENTS = 2
TH = 128
CAP = 32
HIDDEN_SIZE = 98304
HS = 6144


def shard_levels(key, shape, cuts, smallest, high):
    level, own = 1.0, jax.random.fold_in(key, 6)
    for position, shards_of in cuts:
        steps = jnp.exp(jax.random.uniform(jax.random.fold_in(own, position), (shards_of,), jnp.float32, smallest / len(cuts), high / len(cuts)))
        level = level * jnp.repeat(steps, shape[position] // shards_of).reshape([-1 if axis == position else 1 for axis in range(len(shape))])
    return level


def routed_block(rng, own, number, rows, number_of, top, limit, slope):
    sequence = jax.random.permutation(rng, number_of)
    heavy_load, ordinary = portions_of(number_of, rows * top, limit, slope, True), portions_of(number_of, rows * top, limit, slope, False)
    places = jnp.arange(number_of)

    def named(tallies, turn):
        used = int((tallies > 0).sum())
        fixed = max(1, used // 4)
        shifted = fixed + (places - fixed + turn * (used - fixed)) % max(1, number_of - fixed)
        return jnp.zeros((number_of,), jnp.int32).at[sequence[jnp.where(places < fixed, places, shifted)]].set(jnp.asarray(tallies, jnp.int32))

    tallies = jnp.where(number % 4 == 0, named(heavy_load, number // 4), named(ordinary, number - number // 4 - 1))
    mixed = jax.random.permutation(jax.random.fold_in(own, 3), number_of)
    donor, taker = mixed[0:number_of // 2 * 2:2], mixed[1:number_of // 2 * 2:2]
    margin = jnp.minimum(tallies[donor] - 1, limit - tallies[taker]) // 2
    margin = jnp.where((donor == sequence[0]) | (taker == sequence[0]) | (tallies[taker] == 0), 0, jnp.maximum(margin, 0))
    shifted = jax.random.randint(jax.random.fold_in(own, 4), (number_of // 2,), 0, 1 << 20) % (margin + 1)
    tallies = tallies.at[donor].add(-shifted).at[taker].add(shifted)
    members = jnp.searchsorted(jnp.cumsum(tallies), jnp.arange(rows * top), side="right").astype(jnp.int32)
    table = members.reshape(top, rows).T
    table = table[jax.random.permutation(jax.random.fold_in(own, 1), rows)]
    turn = jax.random.randint(jax.random.fold_in(own, 2), (rows, 1), 0, top)
    return jnp.take_along_axis(table, (jnp.arange(top)[None, :] + turn) % top, axis=1)


def portions_of(count, total, limit, slope, full):
    portions = [(1 << 20) // math.isqrt(standing ** slope) + 1 for standing in range(1, count + 1)]
    largest = limit if full else min(limit, max(-(-total // count), total * portions[0] // sum(portions)))
    least = 1 if total - largest >= count - 1 else 0
    holding, surplus = [largest] + [least] * (count - 1), total - largest - least * (count - 1)
    while surplus > 0:
        free = [i for i in range(1, count) if holding[i] < largest] or [i for i in range(1, count) if holding[i] < limit]
        pool, remaining = sum([portions[i] for i in free]), surplus
        for i in free:
            more = min(limit - holding[i], max(1, remaining * portions[i] // pool), surplus)
            holding[i] = holding[i] + more
            surplus = surplus - more
    return np.array(holding)


def gaussian(key, shape, width, bound, cuts=(), kind=jnp.bfloat16):
    array = jax.random.normal(key, shape, jnp.float32) * width
    if len(cuts) > 0:
        array = shard_levels(key, shape, cuts, -0.22, 0.18) * array
    return jnp.clip(array, min=-bound, max=bound).astype(kind)


def setup_inputs(seed: int = 0, part: int = 0) -> dict:
    keys = jax.random.split(jax.random.key(seed), 15)
    own_keys = jax.random.split(jax.random.fold_in(keys[14], part), 15)
    hidden = gaussian(own_keys[0], (LATENTS, SEQ, D), 1.0, 6.0, ((0, 2), (1, 8)))
    modulation = gaussian(own_keys[1], (LATENTS, 3, D), 0.5, 3.0, ((0, 2),), jnp.float32)
    router_weight = gaussian(keys[2], (D, EXPERTS), D ** -0.5, 0.15625, (), jnp.float32)
    route_ids_keys = jax.random.split(jax.random.fold_in(own_keys[3], 1), LATENTS * SEQ // TH)
    route_ids_turns = jax.random.permutation(jax.random.fold_in(own_keys[3], 3), LATENTS * SEQ // TH)
    route_ids = jax.vmap(lambda own, number: routed_block(jax.random.fold_in(own_keys[3], 2), own, number, TH, EXPERTS, TOP, CAP, 2))(route_ids_keys, route_ids_turns).reshape((LATENTS, SEQ, TOP))
    gate_weight = gaussian(keys[4], (D, HIDDEN_SIZE), D ** -0.5, 0.15625, ((1, 16),))
    up_weight = gaussian(keys[5], (D, HIDDEN_SIZE), D ** -0.5, 0.15625, ((1, 16),))
    down_weight = gaussian(keys[6], (HIDDEN_SIZE, D), FF ** -0.5, 0.078125, ((0, 16),))
    main_final = gaussian(keys[7], (D, P_SIZE), D ** -0.5, 0.15625)
    guide_qkv = gaussian(own_keys[8], (LATENTS, SEQ, GH, 3 * HD), 1.0, 6.0, ((0, 2), (1, 4), (2, 2)))
    guide_out = gaussian(keys[9], (GH, HD, DG), DG ** -0.5, 0.3125, ((0, 2),))
    guide_final = gaussian(keys[10], (DG, P_SIZE), DG ** -0.5, 0.3125)
    latent = gaussian(own_keys[11], (LATENTS, SEQ, P_SIZE), 1.0, 6.0, ((0, 2), (1, 8)), jnp.float32)
    guidance = jnp.clip(1.5 + 1.5 * jax.random.uniform(own_keys[12], (LATENTS,), jnp.float32) ** shard_levels(own_keys[12], (LATENTS,), ((0, 2),), -0.2, 0.2), 1.5, 3.0)
    step_size = jnp.clip(0.1 + 0.4 * jax.random.uniform(own_keys[13], (LATENTS,), jnp.float32) ** shard_levels(own_keys[13], (LATENTS,), ((0, 2),), -0.2, 0.2), 0.1, 0.5)
    return dict(hidden=hidden, modulation=modulation, router_weight=router_weight, route_ids=route_ids, gate_weight=gate_weight, up_weight=up_weight, down_weight=down_weight, main_final=main_final, guide_qkv=guide_qkv, guide_out=guide_out, guide_final=guide_final, latent=latent, guidance=guidance, step_size=step_size)


epsilon = 1e-06
score_scale = 8.0

def layer_norm(values):
    average = lax.optimization_barrier(jnp.mean(values, axis=-1, keepdims=True))
    centered = values - average
    return centered / jnp.sqrt(lax.optimization_barrier(jnp.mean(centered * centered, axis=-1, keepdims=True)) + epsilon)

def unit_rows(values):
    return values / jnp.sqrt(lax.optimization_barrier(jnp.mean(values * values, axis=-1, keepdims=True)) + epsilon)

def reference(hidden, modulation, router_weight, route_ids, gate_weight, up_weight, down_weight, main_final, guide_qkv, guide_out, guide_final, latent, guidance, step_size):
    hidden_float = hidden.astype(jnp.float32)
    shift_rows = modulation[:, 0][:, None, :]
    scale_rows = modulation[:, 1][:, None, :]
    gate_rows = modulation[:, 2][:, None, :]
    modulated = (layer_norm(hidden_float) * (1.0 + scale_rows) + shift_rows).astype(jnp.bfloat16)
    token_total = LATENTS * SEQ
    flat_rows = modulated.reshape(token_total, D)
    logits = jnp.dot(flat_rows.astype(jnp.float32), router_weight, precision=lax.Precision.HIGHEST)
    flat_ids = route_ids.reshape(token_total, TOP).astype(jnp.int32)
    picked = jnp.take_along_axis(logits, flat_ids, axis=1)
    first_weight = jax.nn.sigmoid(picked[:, 0] - picked[:, 1])
    route_weight = jnp.stack([first_weight, 1.0 - first_weight], axis=1)
    route_total = token_total * TOP
    route_flat = flat_ids.reshape(route_total)
    row_limit = min(route_total, token_total // TH * CAP)
    block_count = FF // HS

    def one_expert(expert):
        not_mine = (route_flat != expert).astype(jnp.int32)
        order = jnp.argsort(not_mine, stable=True)[:row_limit].astype(jnp.int32)
        valid = (route_flat[order] == expert).astype(jnp.float32)[:, None]
        rows = flat_rows[order // TOP]
        start_unit = expert * FF
        gate_part = lax.dynamic_slice_in_dim(gate_weight, start_unit, FF, 1)
        up_part = lax.dynamic_slice_in_dim(up_weight, start_unit, FF, 1)
        down_part = lax.dynamic_slice_in_dim(down_weight, start_unit, FF, 0)
        gate_vals = jnp.dot(rows, gate_part, preferred_element_type=jnp.float32)
        up_vals = jnp.dot(rows, up_part, preferred_element_type=jnp.float32)
        activated = (jax.nn.silu(gate_vals) * up_vals).astype(jnp.bfloat16)
        blocks = jnp.einsum('rbh,bhd->brd', activated.reshape(row_limit, block_count, HS).astype(jnp.float32), down_part.reshape(block_count, HS, D).astype(jnp.float32))
        rounded = lax.optimization_barrier(blocks.astype(jnp.bfloat16))
        return (lax.optimization_barrier(jnp.sum(rounded.astype(jnp.float32), axis=0)) * valid, order)
    results, orders = lax.map(one_expert, jnp.arange(EXPERTS, dtype=jnp.int32))
    per_route = jnp.zeros((route_total, D), jnp.float32).at[orders.reshape(-1)].add(results.reshape(-1, D))
    moe_out = lax.optimization_barrier(jnp.sum(per_route.reshape(token_total, TOP, D) * route_weight[:, :, None], axis=1))
    updated = hidden_float + gate_rows * moe_out.reshape(LATENTS, SEQ, D)
    main_norm = layer_norm(updated).astype(jnp.bfloat16)
    main_velocity = jnp.dot(main_norm.reshape(token_total, D), main_final, preferred_element_type=jnp.float32).reshape(LATENTS, SEQ, P_SIZE)
    queries = unit_rows(guide_qkv[..., :HD].astype(jnp.float32)).astype(jnp.bfloat16)
    unit_keys = unit_rows(guide_qkv[..., HD:2 * HD].astype(jnp.float32)).astype(jnp.bfloat16)
    values_part = guide_qkv[..., 2 * HD:]

    def one_latent(items):
        query_rows, key_rows, value_rows = items
        scores = jnp.einsum('qhc,khc->hqk', query_rows.astype(jnp.float32), key_rows.astype(jnp.float32)) * (score_scale / HD)
        weights = jnp.exp(scores - score_scale)
        totals = lax.optimization_barrier(jnp.sum(weights, axis=-1))
        rounded = lax.optimization_barrier(weights.astype(jnp.bfloat16))
        mixed = jnp.einsum('hqk,khc->qhc', rounded.astype(jnp.float32), value_rows.astype(jnp.float32))
        return (mixed / jnp.transpose(totals)[:, :, None]).astype(jnp.bfloat16)
    attended = lax.map(one_latent, (queries, unit_keys, values_part))
    guide_mix = jnp.einsum('lqhc,hcd->lqd', attended.astype(jnp.float32), guide_out.astype(jnp.float32))
    guide_norm = layer_norm(guide_mix).astype(jnp.bfloat16)
    guide_velocity = jnp.dot(guide_norm.reshape(token_total, DG), guide_final, preferred_element_type=jnp.float32).reshape(LATENTS, SEQ, P_SIZE)
    guided = guide_velocity + guidance[:, None, None] * (main_velocity - guide_velocity)
    return latent + step_size[:, None, None] * guided
```

```python
import functools

import jax
import jax.numpy as jnp
from jax import lax
from jax.experimental import pallas as pl
from jax.experimental.pallas import tpu as pltpu
from jax.sharding import PartitionSpec as P


FF = 6144
EXPERTS = 16
TOP = 2
HD = 64
P_SIZE = 16


epsilon = 1e-06
score_scale = 8.0
MIB = 1024 * 1024
MEMBERS = ("expert", "dp", "head")
CHUNK_A = [8, 12, 4, 0]
CHUNK_B = [10, 14, 6, 2]


def layer_norm(values):
    average = jnp.mean(values, axis=-1, keepdims=True)
    centered = values - average
    return centered / jnp.sqrt(jnp.mean(centered * centered, axis=-1, keepdims=True) + epsilon)


def unit_rows(values):
    return values / jnp.sqrt(jnp.mean(values * values, axis=-1, keepdims=True) + epsilon)


def prep_kernel(chips, capacity, me_ref, ids_ref, own_ref, other_ref, mod_ref, rows_ref, code_ref, *out_refs):
    tokens = own_ref.shape[1]
    both = 2 * tokens
    for i, ref in enumerate((own_ref, other_ref)):
        rows_ref[i * tokens : (i + 1) * tokens, :] = (
            layer_norm(ref[0].astype(jnp.float32)) * (1.0 + mod_ref[0, 1:2, :]) + mod_ref[0, 0:1, :]
        ).astype(jnp.bfloat16)
    me = me_ref[0]
    experts = lax.broadcasted_iota(jnp.int32, (EXPERTS, both), 0)
    named = [experts == ids_ref[j : j + 1, :] for j in range(TOP)]
    tally = functools.reduce(jnp.logical_or, named).astype(jnp.float32).astype(jnp.bfloat16)
    earlier = lax.broadcasted_iota(jnp.int32, (both, both), 0)
    later = lax.broadcasted_iota(jnp.int32, (both, both), 1)
    before = jnp.logical_and(earlier < later, jnp.logical_or(later < tokens, earlier >= tokens))
    rank = jnp.dot(
        tally, before.astype(jnp.float32).astype(jnp.bfloat16), preferred_element_type=jnp.float32
    )
    second = jnp.where(lax.broadcasted_iota(jnp.int32, (1, both), 1) >= tokens, capacity, 0)
    slots = lax.broadcasted_iota(jnp.int32, (2 * chips * capacity, both), 0)
    hit = None
    for j in range(TOP):
        own_rank = jnp.sum(jnp.where(named[j], rank, 0.0), axis=0, keepdims=True).astype(jnp.int32)
        away = jnp.bitwise_xor(ids_ref[j : j + 1, :], me)
        code = lax.shift_right_logical(away, 1) * (2 * capacity) + second + own_rank
        code = jnp.where(jnp.bitwise_and(away, 1) == 0, code, -1)
        code_ref[j : j + 1, :] = code
        hit = slots == code if hit is None else jnp.logical_or(hit, slots == code)
    select = hit.astype(jnp.float32).astype(jnp.bfloat16)
    for p, out_ref in enumerate(out_refs):
        out_ref[...] = jnp.dot(
            select[2 * p * capacity : 2 * (p + 1) * capacity, :],
            rows_ref[...],
            preferred_element_type=jnp.float32,
        ).astype(jnp.bfloat16)


def prep(me, ids, own, other, modulation, chips, capacity):
    tokens, width = own.shape[1:]
    vmem = pl.BlockSpec(memory_space=pltpu.VMEM)
    return pl.pallas_call(
        functools.partial(prep_kernel, chips, capacity),
        in_specs=[pl.BlockSpec(memory_space=pltpu.SMEM)] + [vmem] * 4,
        out_specs=[vmem] * (2 + chips),
        out_shape=[
            jax.ShapeDtypeStruct((2 * tokens, width), jnp.bfloat16),
            jax.ShapeDtypeStruct((TOP, 2 * tokens), jnp.int32),
        ]
        + [jax.ShapeDtypeStruct((2 * capacity, width), jnp.bfloat16)] * chips,
        compiler_params=pltpu.CompilerParams(vmem_limit_bytes=24 * MIB),
        cost_estimate=pl.CostEstimate(
            flops=8 * chips * capacity * tokens * width,
            bytes_accessed=4 * chips * capacity * width,
            transcendentals=0,
        ),
        name="prep",
    )(me, ids, own, other, modulation)


def ffn_kernel(blocks, *refs):
    row_refs = refs[:blocks]
    gate_ref, up_ref, down_ref = refs[blocks : blocks + 3]
    out_refs = refs[blocks + 3 : 2 * blocks + 3]
    rows, total = refs[2 * blocks + 3 :]
    step, last = pl.program_id(0), pl.num_programs(0) - 1
    capacity = row_refs[0].shape[0]

    @pl.when(step == 0)
    def _():
        for i in range(blocks):
            rows[i * capacity : (i + 1) * capacity, :] = row_refs[i][...]

    gate_vals = jnp.dot(rows[...], gate_ref[...], preferred_element_type=jnp.float32)
    up_vals = jnp.dot(rows[...], up_ref[...], preferred_element_type=jnp.float32)
    activated = (gate_vals / (1.0 + jnp.exp(-gate_vals)) * up_vals).astype(jnp.bfloat16)
    term = jnp.dot(activated, down_ref[...], preferred_element_type=jnp.float32)

    @pl.when(step == 0)
    def _():
        total[...] = term

    @pl.when(jnp.logical_and(step > 0, step < last))
    def _():
        total[...] += term

    @pl.when(step == last)
    def _():
        done = (total[...] + term).astype(jnp.bfloat16)
        for i in range(blocks):
            out_refs[i][...] = done[i * capacity : (i + 1) * capacity, :]


def ffn(row_blocks, gate_weight, up_weight, down_weight):
    blocks = len(row_blocks)
    capacity, width = row_blocks[0].shape
    units = gate_weight.shape[1]
    tile = 1024 if units % 1024 == 0 else units
    rows = blocks * capacity
    whole = pl.BlockSpec((capacity, width), lambda s: (0, 0))
    return pl.pallas_call(
        functools.partial(ffn_kernel, blocks),
        grid=(units // tile,),
        in_specs=[whole] * blocks
        + [
            pl.BlockSpec((width, tile), lambda s: (0, s)),
            pl.BlockSpec((width, tile), lambda s: (0, s)),
            pl.BlockSpec((tile, width), lambda s: (s, 0)),
        ],
        out_specs=[whole] * blocks,
        out_shape=[jax.ShapeDtypeStruct((capacity, width), jnp.bfloat16)] * blocks,
        scratch_shapes=[pltpu.VMEM((rows, width), jnp.bfloat16), pltpu.VMEM((rows, width), jnp.float32)],
        compiler_params=pltpu.CompilerParams(vmem_limit_bytes=56 * MIB),
        cost_estimate=pl.CostEstimate(
            flops=6 * rows * width * units,
            bytes_accessed=6 * width * units,
            transcendentals=rows * units,
        ),
        name="ffn",
    )(*row_blocks, gate_weight, up_weight, down_weight)


def attend_kernel(pieces, head_ref, q_ref, *refs):
    kv_refs = refs[:pieces]
    out_ref, keep_ref, send_ref, mix = refs[pieces:]
    heads, queries = q_ref.shape[:2]
    acc = None
    for h in range(heads):
        q = q_ref[h]
        sums, weighted = None, None
        for kv_ref in kv_refs:
            scores = lax.dot_general(
                q, kv_ref[h, :, :HD], (((1,), (1,)), ((), ())), preferred_element_type=jnp.float32
            ) * (score_scale / HD)
            weights = jnp.exp(scores - score_scale)
            part = jnp.sum(weights, axis=-1, keepdims=True)
            value = jnp.dot(
                weights.astype(jnp.bfloat16), kv_ref[h, :, HD:], preferred_element_type=jnp.float32
            )
            sums = part if sums is None else sums + part
            weighted = value if weighted is None else weighted + value
        attended = (weighted / sums).astype(jnp.bfloat16)
        term = jnp.dot(attended, out_ref[h], preferred_element_type=jnp.float32)
        acc = term if acc is None else acc + term
    mix[...] = acc
    half = queries // 2
    mine = head_ref[0]
    keep_ref[...] = mix[pl.ds(pl.multiple_of(mine * half, half), half), :]
    send_ref[...] = mix[pl.ds(pl.multiple_of((1 - mine) * half, half), half), :].astype(jnp.bfloat16)


def attend(head, queries, kv_pieces, guide_out):
    heads, count, _ = queries.shape
    keys = sum(piece.shape[1] for piece in kv_pieces)
    wide = guide_out.shape[-1]
    vmem = pl.BlockSpec(memory_space=pltpu.VMEM)
    return pl.pallas_call(
        functools.partial(attend_kernel, len(kv_pieces)),
        in_specs=[pl.BlockSpec(memory_space=pltpu.SMEM)] + [vmem] * (2 + len(kv_pieces)),
        out_specs=[vmem, vmem],
        out_shape=[
            jax.ShapeDtypeStruct((count // 2, wide), jnp.float32),
            jax.ShapeDtypeStruct((count // 2, wide), jnp.bfloat16),
        ],
        scratch_shapes=[pltpu.VMEM((count, wide), jnp.float32)],
        compiler_params=pltpu.CompilerParams(vmem_limit_bytes=32 * MIB),
        cost_estimate=pl.CostEstimate(
            flops=4 * heads * count * keys * HD,
            bytes_accessed=4 * heads * keys * HD,
            transcendentals=heads * count * keys,
        ),
        name="attend",
    )(head, queries, *kv_pieces, guide_out)


def combine_kernel(blocks, code_ref, first_ref, *refs):
    row_refs, (keep_ref, send_ref, rows) = refs[:blocks], refs[blocks:]
    size = row_refs[0].shape[0]
    for i in range(blocks):
        rows[i * size : (i + 1) * size, :] = row_refs[i][...]
    both = code_ref.shape[0]
    tokens = both // 2
    slots = lax.broadcasted_iota(jnp.int32, (tokens, blocks * size), 1)
    for i, out_ref in enumerate((keep_ref, send_ref)):
        part = slice(i * tokens, (i + 1) * tokens)
        first = first_ref[part, :]
        total = None
        for j, weight in enumerate((first, 1.0 - first)):
            pick = (slots == code_ref[part, j : j + 1]).astype(jnp.float32).astype(jnp.bfloat16)
            term = weight * jnp.dot(pick, rows[...], preferred_element_type=jnp.float32)
            total = term if total is None else total + term
        out_ref[...] = total.astype(out_ref.dtype)


def combine(row_blocks, code, first):
    blocks = len(row_blocks)
    size, width = row_blocks[0].shape
    tokens = code.shape[0] // 2
    vmem = pl.BlockSpec(memory_space=pltpu.VMEM)
    return pl.pallas_call(
        functools.partial(combine_kernel, blocks),
        in_specs=[vmem] * (2 + blocks),
        out_specs=[vmem] * 2,
        out_shape=[
            jax.ShapeDtypeStruct((tokens, width), jnp.float32),
            jax.ShapeDtypeStruct((tokens, width), jnp.bfloat16),
        ],
        scratch_shapes=[pltpu.VMEM((blocks * size, width), jnp.bfloat16)],
        compiler_params=pltpu.CompilerParams(vmem_limit_bytes=24 * MIB),
        cost_estimate=pl.CostEstimate(
            flops=8 * tokens * blocks * size * width,
            bytes_accessed=2 * blocks * size * width,
            transcendentals=0,
        ),
        name="combine",
    )(code, first, *row_blocks)


def finish_kernel(
    keep_moe_ref, got_moe_ref, hidden_ref, mod_ref, final_ref, keep_ref, got_ref, guide_final_ref, latent_ref,
    guidance_ref, step_ref, out_ref
):
    moe_out = keep_moe_ref[...] + got_moe_ref[...].astype(jnp.float32)
    updated = hidden_ref[0].astype(jnp.float32) + mod_ref[0, 2:3, :] * moe_out
    main_velocity = jnp.dot(
        layer_norm(updated).astype(jnp.bfloat16), final_ref[...], preferred_element_type=jnp.float32
    )
    guide_mix = keep_ref[...] + got_ref[...].astype(jnp.float32)
    guide_velocity = jnp.dot(
        layer_norm(guide_mix).astype(jnp.bfloat16), guide_final_ref[...], preferred_element_type=jnp.float32
    )
    guided = guide_velocity + guidance_ref[0] * (main_velocity - guide_velocity)
    out_ref[0] = latent_ref[0] + step_ref[0] * guided


def finish(keep_moe, got_moe, hidden, modulation, main_final, keep, got, guide_final, latent, guidance, step_size):
    vmem = pl.BlockSpec(memory_space=pltpu.VMEM)
    smem = pl.BlockSpec(memory_space=pltpu.SMEM)
    return pl.pallas_call(
        finish_kernel,
        in_specs=[vmem] * 9 + [smem] * 2,
        out_specs=vmem,
        out_shape=jax.ShapeDtypeStruct(latent.shape, latent.dtype),
        compiler_params=pltpu.CompilerParams(vmem_limit_bytes=16 * MIB),
        cost_estimate=pl.CostEstimate(flops=hidden.size * 64, bytes_accessed=hidden.size * 8, transcendentals=0),
        name="finish",
    )(keep_moe, got_moe, hidden, modulation, main_final, keep, got, guide_final, latent, guidance, step_size)


def direct_body(
    hidden,
    modulation,
    router_weight,
    route_ids,
    gate_weight,
    up_weight,
    down_weight,
    main_final,
    guide_qkv,
    guide_out,
    guide_final,
    latent,
    guidance,
    step_size,
):
    return direct_step(
        hidden, modulation, router_weight, route_ids, gate_weight, up_weight, down_weight, main_final,
        guide_qkv, guide_out, guide_final, latent, guidance, step_size,
    )


def direct_step(
    hidden, modulation, router_weight, route_ids, gate_weight, up_weight, down_weight, main_final, guide_qkv,
    guide_out, guide_final, latent, guidance, step_size,
):
    tokens = hidden.shape[1]
    devices = lax.axis_size(MEMBERS)
    capacity = max(2, 2 * tokens * TOP // EXPERTS)
    me = lax.axis_index(MEMBERS).astype(jnp.int32)[None]
    head = lax.axis_index("head").astype(jnp.int32)[None]

    def swap(block, k):
        if k == 0:
            return block
        return lax.ppermute(block, MEMBERS, [(i, i ^ k) for i in range(devices)])

    other = swap(hidden, 1)
    ids = route_ids[0].T
    ids = jnp.concatenate([ids, swap(ids, 1)], axis=1)
    rows, code, *outgoing = prep(me, ids, hidden, other, modulation, devices // 2, capacity)
    rows_a = [swap(outgoing[k // 2], k) for k in CHUNK_A]

    qkv = jnp.transpose(guide_qkv[0], (1, 0, 2))
    queries = unit_rows(qkv[..., :HD].astype(jnp.float32)).astype(jnp.bfloat16)
    keys = unit_rows(qkv[..., HD : 2 * HD].astype(jnp.float32)).astype(jnp.bfloat16)
    kv = jnp.concatenate([keys, qkv[..., 2 * HD :]], axis=-1)
    logits = jnp.dot(rows.astype(jnp.float32), router_weight, precision=lax.Precision.HIGHEST)
    named = jnp.arange(EXPERTS, dtype=jnp.int32)[None, :]
    picked = [
        jnp.sum(jnp.where(ids[j][:, None] == named, logits, 0.0), axis=1, keepdims=True) for j in range(TOP)
    ]
    first = jax.nn.sigmoid(picked[0] - picked[1])
    slot_codes = code.T

    rows_a, second, kv, first, slot_codes, queries = lax.optimization_barrier(
        (rows_a, [outgoing[k // 2] for k in CHUNK_B], kv, first, slot_codes, queries)
    )
    rows_b = [swap(block, k) for block, k in zip(second, CHUNK_B)]
    near = swap(kv, 4)

    done_a = ffn(rows_a, gate_weight, up_weight, down_weight)
    done_a, kv_far = lax.optimization_barrier((done_a, kv))
    back_a = [swap(block, k) for block, k in zip(done_a, CHUNK_A)]
    far = swap(kv_far, 8)

    done_b = ffn(rows_b, gate_weight, up_weight, down_weight)
    done_b, far, near, queries = lax.optimization_barrier((done_b, far, near, queries))
    back_b = [swap(block, k) for block, k in zip(done_b, CHUNK_B)]
    relayed = swap(far, 4)

    keep, send = attend(head, queries, [kv, near, far, relayed], guide_out)
    got = swap(send, 1)

    back = dict(zip(CHUNK_A + CHUNK_B, back_a + back_b))
    keep_moe, send_moe = combine([back[k] for k in sorted(back)], slot_codes, first)
    got_moe = swap(send_moe, 1)
    return finish(
        keep_moe, got_moe, hidden, modulation, main_final, keep, got, guide_final, latent, guidance, step_size
    )


def route_slots(flat_ids, block_slots, per_index, copies):
    route_flat = flat_ids.reshape(-1)
    one_hot = (route_flat[:, None] == jnp.arange(EXPERTS, dtype=jnp.int32)[None, :]).astype(
        jnp.int32
    )
    earlier = jnp.cumsum(one_hot, axis=0) - one_hot
    earlier_count = jnp.sum(earlier * one_hot, axis=1)
    slot_pos = route_flat % per_index * block_slots + earlier_count
    targets = (
        route_flat[:, None] * copies + jnp.arange(copies, dtype=jnp.int32)[None, :]
    ) // per_index
    return (targets, slot_pos)


def expert_hidden(
    rows, positions, gate_weight, up_weight, my_expert, index_first, block_slots, copies
):
    owner_expert = (index_first + positions // block_slots) // copies
    keep_mask = (owner_expert == my_expert).astype(jnp.float32)[:, None]
    gate_vals = jnp.dot(rows, gate_weight, preferred_element_type=jnp.float32)
    up_vals = jnp.dot(rows, up_weight, preferred_element_type=jnp.float32)
    return (jax.nn.silu(gate_vals) * up_vals * keep_mask).astype(jnp.bfloat16)


def spread_body(
    hidden,
    modulation,
    router_weight,
    route_ids,
    gate_weight,
    up_weight,
    down_weight,
    main_final,
    guide_qkv,
    guide_out,
    guide_final,
    latent,
    guidance,
    step_size,
):
    lat_dev, tok_dev, width = hidden.shape
    experts_axis = lax.axis_size("expert")
    group_size = lax.axis_size(("dp", "head"))
    slice_units = gate_weight.shape[1]
    index_units = slice_units * group_size
    if EXPERTS >= experts_axis:
        per_index = EXPERTS // experts_axis
        copies = 1
    else:
        per_index = 1
        copies = experts_axis // EXPERTS
    capacity = max(2, 2 * tok_dev * TOP // EXPERTS)
    block_slots = lat_dev * capacity
    slot_count = per_index * block_slots
    my_index = lax.axis_index("expert")
    my_member = lax.axis_index(("dp", "head"))
    my_expert = (my_index * index_units + my_member * slice_units) // FF
    index_first = my_index * per_index
    hidden_float = hidden.astype(jnp.float32)
    modulated = (
        layer_norm(hidden_float) * (1.0 + modulation[:, 1][:, None, :])
        + modulation[:, 0][:, None, :]
    ).astype(jnp.bfloat16)
    row_count = lat_dev * tok_dev
    flat_rows = modulated.reshape(row_count, width)
    logits = jnp.dot(flat_rows.astype(jnp.float32), router_weight, precision=lax.Precision.HIGHEST)
    flat_ids = route_ids.reshape(row_count, TOP)
    picked = jnp.take_along_axis(logits, flat_ids, axis=1)
    first_weight = jax.nn.sigmoid(picked[:, 0] - picked[:, 1])
    route_weight = jnp.stack([first_weight, 1.0 - first_weight], axis=1)
    route_count = row_count * TOP
    route_token = jnp.arange(route_count, dtype=jnp.int32) // TOP
    targets, slot_pos = route_slots(flat_ids, block_slots, per_index, copies)
    outgoing = jnp.zeros((experts_axis, slot_count, width), jnp.bfloat16)
    payload = jnp.broadcast_to(flat_rows[route_token][:, None, :], (route_count, copies, width))
    outgoing = outgoing.at[targets, slot_pos[:, None]].set(payload)
    received = lax.all_to_all(outgoing, "expert", split_axis=0, concat_axis=0, tiled=True)
    received_rows = received.reshape(experts_axis * slot_count, width)
    piece = lax.all_gather(received_rows, ("dp", "head"), axis=0, tiled=True)
    positions = jnp.arange(piece.shape[0], dtype=jnp.int32) % slot_count
    activated = expert_hidden(
        piece, positions, gate_weight, up_weight, my_expert, index_first, block_slots, copies
    )
    term = jnp.dot(activated, down_weight, preferred_element_type=jnp.float32)
    row_sums = lax.psum_scatter(
        lax.optimization_barrier(term.astype(jnp.bfloat16))
        .astype(jnp.float32)
        .astype(jnp.bfloat16),
        ("dp", "head"),
        scatter_dimension=0,
        tiled=True,
    ).astype(jnp.float32)
    returned = lax.all_to_all(
        row_sums.reshape(experts_axis, slot_count, width).astype(jnp.bfloat16),
        "expert",
        split_axis=0,
        concat_axis=0,
        tiled=True,
    ).astype(jnp.float32)
    gathered_back = returned[targets, slot_pos[:, None]]
    per_route = jnp.sum(gathered_back, axis=1).reshape(row_count, TOP, width)
    moe_out = jnp.sum(per_route * route_weight[:, :, None], axis=1)
    updated = hidden_float + modulation[:, 2][:, None, :] * moe_out.reshape(lat_dev, tok_dev, width)
    main_norm = layer_norm(updated).astype(jnp.bfloat16)
    main_velocity = jnp.dot(
        main_norm.reshape(row_count, width), main_final, preferred_element_type=jnp.float32
    ).reshape(lat_dev, tok_dev, P_SIZE)
    queries = unit_rows(guide_qkv[..., :HD].astype(jnp.float32)).astype(jnp.bfloat16)
    unit_keys = unit_rows(guide_qkv[..., HD : 2 * HD].astype(jnp.float32)).astype(jnp.bfloat16)
    key_value = jnp.concatenate([unit_keys, guide_qkv[..., 2 * HD :]], axis=-1)
    piece = lax.all_gather(key_value, "expert", axis=1, tiled=True)
    key_piece = piece[..., :HD]
    value_piece = piece[..., HD:]
    scores = jnp.einsum(
        "lqhc,lkhc->lhqk", queries, key_piece, preferred_element_type=jnp.float32
    ) * (score_scale / HD)
    weights = jnp.exp(scores - score_scale)
    weighted_sum = jnp.einsum(
        "lhqk,lkhc->lqhc",
        weights.astype(jnp.bfloat16),
        value_piece,
        preferred_element_type=jnp.float32,
    )
    weight_total = jnp.transpose(jnp.sum(weights, axis=-1), (0, 2, 1))
    attended = (weighted_sum / weight_total[..., None]).astype(jnp.bfloat16)
    partial_mix = jnp.einsum(
        "lqhc,hcd->lqd", attended, guide_out, preferred_element_type=jnp.float32
    )
    guide_mix = lax.psum_scatter(
        partial_mix.astype(jnp.bfloat16), "head", scatter_dimension=1, tiled=True
    ).astype(jnp.float32)
    guide_norm = layer_norm(guide_mix).astype(jnp.bfloat16)
    guide_width = guide_norm.shape[-1]
    guide_velocity = jnp.dot(
        guide_norm.reshape(row_count, guide_width), guide_final, preferred_element_type=jnp.float32
    ).reshape(lat_dev, tok_dev, P_SIZE)
    guided = guide_velocity + guidance[:, None, None] * (main_velocity - guide_velocity)
    return latent + step_size[:, None, None] * guided


def solution(mesh):
    in_specs = (
        P(("groups", "dp"), ("expert", "head"), None),
        P(("groups", "dp"), None, None),
        P(),
        P(("groups", "dp"), ("expert", "head"), None),
        P(None, ("expert", "dp", "head")),
        P(None, ("expert", "dp", "head")),
        P(("expert", "dp", "head"), None),
        P(),
        P(("groups", "dp"), "expert", "head", None),
        P("head", None, None),
        P(),
        P(("groups", "dp"), ("expert", "head"), None),
        P(("groups", "dp")),
        P(("groups", "dp")),
    )
    out_specs = P(("groups", "dp"), ("expert", "head"), None)
    sizes = dict(mesh.shape)
    members = sizes["expert"] * sizes["dp"] * sizes["head"]
    direct = members == EXPERTS and sizes["expert"] == 4 and sizes["head"] == 2
    body = direct_body if direct else spread_body
    return jax.shard_map(body, mesh=mesh, in_specs=in_specs, out_specs=out_specs, check_vma=False)
```

```python
import functools

import jax
import jax.numpy as jnp
from jax import lax
from jax.experimental import pallas as pl
from jax.experimental.pallas import tpu as pltpu
from jax.sharding import PartitionSpec as P


FF = 6144
EXPERTS = 16
TOP = 2
HD = 64
P_SIZE = 16


epsilon = 1e-06
score_scale = 8.0
MIB = 1024 * 1024
MEMBERS = ("expert", "dp", "head")
CHUNK_A = [8, 12, 4, 0]
CHUNK_B = [2, 6, 10, 14]


def layer_norm(values):
    average = jnp.mean(values, axis=-1, keepdims=True)
    centered = values - average
    return centered / jnp.sqrt(jnp.mean(centered * centered, axis=-1, keepdims=True) + epsilon)


def unit_rows(values):
    return values / jnp.sqrt(jnp.mean(values * values, axis=-1, keepdims=True) + epsilon)


def modulate(values, mod_ref):
    return (layer_norm(values.astype(jnp.float32)) * (1.0 + mod_ref[1]) + mod_ref[0]).astype(jnp.bfloat16)


def fetch(pairs, sems):
    copies = [pltpu.make_async_copy(src, dst, sems.at[i]) for i, (src, dst) in enumerate(pairs)]
    for copy in copies:
        copy.start()
    for copy in copies:
        copy.wait()


def own_rows_kernel(own_hbm, mod_hbm, rows_ref, own, mod, sems):
    fetch([(own_hbm, own), (mod_hbm, mod)], sems)
    rows_ref[...] = modulate(own[0], mod)


def own_rows(own, modulation):
    hbm = pl.BlockSpec(memory_space=pl.ANY)
    return pl.pallas_call(
        own_rows_kernel,
        in_specs=[hbm] * 2,
        out_specs=pl.BlockSpec(memory_space=pltpu.VMEM),
        out_shape=jax.ShapeDtypeStruct(own.shape[1:], jnp.bfloat16),
        scratch_shapes=[
            pltpu.VMEM(own.shape, own.dtype),
            pltpu.VMEM(modulation.shape, modulation.dtype),
            pltpu.SemaphoreType.DMA((2,)),
        ],
        compiler_params=pltpu.CompilerParams(vmem_limit_bytes=16 * MIB),
        cost_estimate=pl.CostEstimate(flops=8 * own.size, bytes_accessed=4 * own.size, transcendentals=0),
        name="own_rows",
    )(own, modulation)


def prep_kernel(
    chips, capacity, me_ref, own_ids_hbm, other_ids_hbm, own_rows_ref, other_hbm, mod_hbm, rows_ref, code_ref, *refs
):
    out_refs, (own_ids, other_ids, other, mod, sems) = refs[:chips], refs[chips:]
    tokens = own_rows_ref.shape[0]
    both = 2 * tokens
    fetch(
        [(own_ids_hbm, own_ids), (other_ids_hbm, other_ids), (other_hbm, other), (mod_hbm, mod)], sems
    )
    rows_ref[:tokens, :] = own_rows_ref[...]
    rows_ref[tokens:, :] = modulate(other[0], mod)
    me = me_ref[0]
    ids = jnp.concatenate([own_ids[0], other_ids[0]], axis=1)
    experts = lax.broadcasted_iota(jnp.int32, (EXPERTS, both), 0)
    named = [experts == ids[j : j + 1, :] for j in range(TOP)]
    tally = functools.reduce(jnp.logical_or, named).astype(jnp.float32).astype(jnp.bfloat16)
    earlier = lax.broadcasted_iota(jnp.int32, (both, both), 0)
    later = lax.broadcasted_iota(jnp.int32, (both, both), 1)
    before = jnp.logical_and(earlier < later, jnp.logical_or(later < tokens, earlier >= tokens))
    rank = jnp.dot(
        tally, before.astype(jnp.float32).astype(jnp.bfloat16), preferred_element_type=jnp.float32
    )
    second = jnp.where(lax.broadcasted_iota(jnp.int32, (1, both), 1) >= tokens, capacity, 0)
    slots = lax.broadcasted_iota(jnp.int32, (2 * chips * capacity, both), 0)
    hit = None
    for j in range(TOP):
        own_rank = jnp.sum(jnp.where(named[j], rank, 0.0), axis=0, keepdims=True).astype(jnp.int32)
        away = jnp.bitwise_xor(ids[j : j + 1, :], me)
        code = lax.shift_right_logical(away, 1) * (2 * capacity) + second + own_rank
        code = jnp.where(jnp.bitwise_and(away, 1) == 0, code, -1)
        code_ref[j : j + 1, :] = code
        hit = slots == code if hit is None else jnp.logical_or(hit, slots == code)
    select = hit.astype(jnp.float32).astype(jnp.bfloat16)
    for p, out_ref in enumerate(out_refs):
        out_ref[...] = jnp.dot(
            select[2 * p * capacity : 2 * (p + 1) * capacity, :],
            rows_ref[...],
            preferred_element_type=jnp.float32,
        ).astype(jnp.bfloat16)


def prep(me, own_ids, other_ids, rows, other, modulation, chips, capacity):
    tokens, width = rows.shape
    vmem, hbm = pl.BlockSpec(memory_space=pltpu.VMEM), pl.BlockSpec(memory_space=pl.ANY)
    return pl.pallas_call(
        functools.partial(prep_kernel, chips, capacity),
        in_specs=[pl.BlockSpec(memory_space=pltpu.SMEM), hbm, hbm, vmem, hbm, hbm],
        out_specs=[vmem] * (2 + chips),
        out_shape=[
            jax.ShapeDtypeStruct((2 * tokens, width), jnp.bfloat16),
            jax.ShapeDtypeStruct((TOP, 2 * tokens), jnp.int32),
        ]
        + [jax.ShapeDtypeStruct((2 * capacity, width), jnp.bfloat16)] * chips,
        scratch_shapes=[
            pltpu.VMEM(own_ids.shape, own_ids.dtype),
            pltpu.VMEM(other_ids.shape, other_ids.dtype),
            pltpu.VMEM(other.shape, other.dtype),
            pltpu.VMEM(modulation.shape, modulation.dtype),
            pltpu.SemaphoreType.DMA((4,)),
        ],
        compiler_params=pltpu.CompilerParams(vmem_limit_bytes=16 * MIB),
        cost_estimate=pl.CostEstimate(
            flops=8 * chips * capacity * tokens * width,
            bytes_accessed=4 * chips * capacity * width,
            transcendentals=0,
        ),
        name="prep",
    )(me, own_ids, other_ids, rows, other, modulation)


RESIDENT = 1


def weight_tile(units):
    return 768 if units % 768 == 0 else 128


def resident_kernel(gate_hbm, up_hbm, down_hbm, gate_ref, up_ref, down_ref, sems):
    part = pl.ds(0, gate_ref.shape[1])
    fetch(
        [(gate_hbm.at[:, part], gate_ref), (up_hbm.at[:, part], up_ref), (down_hbm.at[part, :], down_ref)], sems
    )


def resident(gate_weight, up_weight, down_weight):
    width, units = gate_weight.shape
    kept = RESIDENT * weight_tile(units)
    vmem, hbm = pl.BlockSpec(memory_space=pltpu.VMEM), pl.BlockSpec(memory_space=pl.ANY)
    return pl.pallas_call(
        resident_kernel,
        in_specs=[hbm] * 3,
        out_specs=[vmem] * 3,
        out_shape=[
            jax.ShapeDtypeStruct((width, kept), jnp.bfloat16),
            jax.ShapeDtypeStruct((width, kept), jnp.bfloat16),
            jax.ShapeDtypeStruct((kept, width), jnp.bfloat16),
        ],
        scratch_shapes=[pltpu.SemaphoreType.DMA((3,))],
        compiler_params=pltpu.CompilerParams(vmem_limit_bytes=46 * MIB),
        cost_estimate=pl.CostEstimate(flops=0, bytes_accessed=6 * width * kept, transcendentals=0),
        name="resident",
    )(gate_weight, up_weight, down_weight)


def ffn_kernel(blocks, tiles, *refs):
    row_refs = refs[:blocks]
    kept_gate, kept_up, kept_down, gate_hbm, up_hbm, down_hbm = refs[blocks : blocks + 6]
    out_refs = refs[blocks + 6 : 2 * blocks + 6]
    rows, total, hidden, gate, up, down, sems = refs[2 * blocks + 6 :]
    size = row_refs[0].shape[0]
    slots, tile = down.shape[0], down.shape[1]

    def copies(step):
        slot, part = lax.rem(step, slots), pl.ds(pl.multiple_of(step * tile, tile), tile)
        return (
            pltpu.make_async_copy(gate_hbm.at[:, part], gate.at[slot], sems.at[0, slot]),
            pltpu.make_async_copy(up_hbm.at[:, part], up.at[slot], sems.at[1, slot]),
            pltpu.make_async_copy(down_hbm.at[part, :], down.at[slot], sems.at[2, slot]),
        )

    def start(step):
        for copy in copies(step):
            copy.start()

    def units_of(gate_tile, up_tile):
        gate_vals = jnp.dot(rows[...], gate_tile, preferred_element_type=jnp.float32)
        up_vals = jnp.dot(rows[...], up_tile, preferred_element_type=jnp.float32)
        return gate_vals, up_vals

    def activate(gate_vals, up_vals):
        return (gate_vals / (1.0 + jnp.exp(-gate_vals)) * up_vals).astype(jnp.bfloat16)

    def part_of(step):
        return slice(step * tile, (step + 1) * tile)

    for step in range(RESIDENT, min(RESIDENT + slots, tiles)):
        start(jnp.int32(step))
    for i in range(blocks):
        rows[i * size : (i + 1) * size, :] = row_refs[i][...]
    hidden[0] = activate(*units_of(kept_gate[:, part_of(0)], kept_up[:, part_of(0)]))

    for step in range(1, RESIDENT):
        vals = units_of(kept_gate[:, part_of(step)], kept_up[:, part_of(step)])
        term = jnp.dot(hidden[(step - 1) % 2], kept_down[part_of(step - 1), :], preferred_element_type=jnp.float32)
        total[...] = term if step == 1 else total[...] + term
        hidden[step % 2] = activate(*vals)

    def wait_units(step):
        gate_copy, up_copy, _ = copies(step)
        gate_copy.wait()
        up_copy.wait()

    wait_units(jnp.int32(RESIDENT))
    vals = units_of(gate[RESIDENT % slots], up[RESIDENT % slots])
    term = jnp.dot(
        hidden[(RESIDENT - 1) % 2], kept_down[part_of(RESIDENT - 1), :], preferred_element_type=jnp.float32
    )
    total[...] = term if RESIDENT == 1 else total[...] + term
    hidden[RESIDENT % 2] = activate(*vals)

    def body(step, carry):
        slot, last = lax.rem(step, slots), lax.rem(step - 1, slots)
        wait_units(step)
        copies(step - 1)[2].wait()
        now = lax.rem(step, 2)
        vals = units_of(gate[slot], up[slot])
        total[...] += jnp.dot(hidden[1 - now], down[last], preferred_element_type=jnp.float32)
        hidden[now] = activate(*vals)

        @pl.when(step + slots - 1 < tiles)
        def _():
            start(step + slots - 1)

        return carry

    lax.fori_loop(RESIDENT + 1, tiles, body, 0)
    copies(jnp.int32(tiles - 1))[2].wait()
    done = total[...] + jnp.dot(
        hidden[(tiles - 1) % 2], down[(tiles - 1) % slots], preferred_element_type=jnp.float32
    )
    for i in range(blocks):
        out_refs[i][...] = done[i * size : (i + 1) * size, :].astype(jnp.bfloat16)


def ffn(row_blocks, kept, gate_weight, up_weight, down_weight):
    blocks = len(row_blocks)
    size, width = row_blocks[0].shape
    units = gate_weight.shape[1]
    tile = weight_tile(units)
    rows, slots = blocks * size, 3
    vmem, hbm = pl.BlockSpec(memory_space=pltpu.VMEM), pl.BlockSpec(memory_space=pl.ANY)
    return pl.pallas_call(
        functools.partial(ffn_kernel, blocks, units // tile),
        in_specs=[vmem] * (blocks + 3) + [hbm] * 3,
        out_specs=[vmem] * blocks,
        out_shape=[jax.ShapeDtypeStruct((size, width), jnp.bfloat16)] * blocks,
        scratch_shapes=[
            pltpu.VMEM((rows, width), jnp.bfloat16),
            pltpu.VMEM((rows, width), jnp.float32),
            pltpu.VMEM((2, rows, tile), jnp.bfloat16),
            pltpu.VMEM((slots, width, tile), jnp.bfloat16),
            pltpu.VMEM((slots, width, tile), jnp.bfloat16),
            pltpu.VMEM((slots, tile, width), jnp.bfloat16),
            pltpu.SemaphoreType.DMA((3, slots)),
        ],
        compiler_params=pltpu.CompilerParams(vmem_limit_bytes=36 * MIB),
        cost_estimate=pl.CostEstimate(
            flops=6 * rows * width * units,
            bytes_accessed=6 * width * units,
            transcendentals=rows * units,
        ),
        name="ffn",
    )(*row_blocks, *kept, gate_weight, up_weight, down_weight)


def side_kernel(
    rows_ref, router_hbm, own_ids_hbm, other_ids_hbm, code_ref, qkv_hbm, q_ref, kv_ref, routes_ref, router_ref,
    own_ids_ref, other_ids_ref, qkv, sems
):
    copy = pltpu.make_async_copy(qkv_hbm, qkv, sems.at[3])
    copy.start()
    fetch([(router_hbm, router_ref), (own_ids_hbm, own_ids_ref), (other_ids_hbm, other_ids_ref)], sems)
    logits = lax.dot_general(
        router_ref[...],
        rows_ref[...].astype(jnp.float32),
        (((1,), (1,)), ((), ())),
        precision=lax.Precision.HIGHEST,
        preferred_element_type=jnp.float32,
    )
    ids = jnp.concatenate([own_ids_ref[0], other_ids_ref[0]], axis=1)
    experts = lax.broadcasted_iota(jnp.int32, logits.shape, 0)
    picked = [
        jnp.sum(jnp.where(experts == ids[j : j + 1, :], logits, 0.0), axis=0, keepdims=True)
        for j in range(TOP)
    ]
    first = 1.0 / (1.0 + jnp.exp(picked[1] - picked[0]))
    line = lax.broadcasted_iota(jnp.int32, (8, first.shape[1]), 0)
    table = jnp.where(line == 0, first, 0.0)
    for j in range(TOP):
        table = jnp.where(line == j + 1, code_ref[j : j + 1, :].astype(jnp.float32), table)
    routes_ref[...] = jnp.transpose(table)

    def unit(values):
        return (
            values / jnp.sqrt(jnp.mean(values * values, axis=0, keepdims=True) + epsilon)
        ).astype(jnp.bfloat16)

    copy.wait()
    for h in range(qkv.shape[0]):
        q_ref[h] = unit(qkv[h, :HD, :].astype(jnp.float32))
        kv_ref[h, :HD, :] = unit(qkv[h, HD : 2 * HD, :].astype(jnp.float32))
        kv_ref[h, HD:, :] = qkv[h, 2 * HD :, :]


def side(rows, router, own_ids, other_ids, code, qkv):
    heads, _, tokens = qkv.shape
    vmem, hbm = pl.BlockSpec(memory_space=pltpu.VMEM), pl.BlockSpec(memory_space=pl.ANY)
    return pl.pallas_call(
        side_kernel,
        in_specs=[vmem, hbm, hbm, hbm, vmem, hbm],
        out_specs=[vmem] * 3,
        out_shape=[
            jax.ShapeDtypeStruct((heads, HD, tokens), jnp.bfloat16),
            jax.ShapeDtypeStruct((heads, 2 * HD, tokens), jnp.bfloat16),
            jax.ShapeDtypeStruct((rows.shape[0], 8), jnp.float32),
        ],
        scratch_shapes=[
            pltpu.VMEM(router.shape, router.dtype),
            pltpu.VMEM(own_ids.shape, own_ids.dtype),
            pltpu.VMEM(other_ids.shape, other_ids.dtype),
            pltpu.VMEM(qkv.shape, qkv.dtype),
            pltpu.SemaphoreType.DMA((4,)),
        ],
        compiler_params=pltpu.CompilerParams(vmem_limit_bytes=16 * MIB),
        cost_estimate=pl.CostEstimate(
            flops=6 * qkv.size + 12 * rows.size * EXPERTS, bytes_accessed=4 * qkv.size, transcendentals=0
        ),
        name="side",
    )(rows, router, own_ids, other_ids, code, qkv)


def attend_kernel(pieces, head_ref, q_ref, *refs):
    kv_refs = refs[:pieces]
    out_ref, keep_ref, send_ref, mix = refs[pieces:]
    heads, _, queries = q_ref.shape
    for h in range(heads):
        sums, weighted = None, None
        for kv_ref in kv_refs:
            scores = lax.dot_general(
                kv_ref[h, :HD, :], q_ref[h], (((0,), (0,)), ((), ())), preferred_element_type=jnp.float32
            ) * (score_scale / HD)
            weights = jnp.exp(scores - score_scale)
            part = jnp.sum(weights, axis=0, keepdims=True)
            value = jnp.dot(
                kv_ref[h, HD:, :], weights.astype(jnp.bfloat16), preferred_element_type=jnp.float32
            )
            sums = part if sums is None else sums + part
            weighted = value if weighted is None else weighted + value
        attended = (weighted / sums).astype(jnp.bfloat16)
        term = lax.dot_general(
            attended, out_ref[h], (((0,), (0,)), ((), ())), preferred_element_type=jnp.float32
        )
        if h == 0:
            mix[...] = term
        else:
            mix[...] += term
    half = queries // 2
    mine = head_ref[0]
    keep_ref[...] = mix[pl.ds(pl.multiple_of(mine * half, half), half), :]
    send_ref[...] = mix[pl.ds(pl.multiple_of((1 - mine) * half, half), half), :].astype(jnp.bfloat16)


def attend(head, queries, kv_pieces, guide_out):
    heads, _, count = queries.shape
    keys = sum(piece.shape[2] for piece in kv_pieces)
    wide = guide_out.shape[-1]
    vmem = pl.BlockSpec(memory_space=pltpu.VMEM)
    return pl.pallas_call(
        functools.partial(attend_kernel, len(kv_pieces)),
        in_specs=[pl.BlockSpec(memory_space=pltpu.SMEM)] + [vmem] * (2 + len(kv_pieces)),
        out_specs=[vmem, vmem],
        out_shape=[
            jax.ShapeDtypeStruct((count // 2, wide), jnp.float32),
            jax.ShapeDtypeStruct((count // 2, wide), jnp.bfloat16),
        ],
        scratch_shapes=[pltpu.VMEM((count, wide), jnp.float32)],
        compiler_params=pltpu.CompilerParams(vmem_limit_bytes=16 * MIB),
        cost_estimate=pl.CostEstimate(
            flops=4 * heads * count * keys * HD,
            bytes_accessed=4 * heads * keys * HD,
            transcendentals=heads * count * keys,
        ),
        name="attend",
    )(head, queries, *kv_pieces, guide_out)


def combine_kernel(blocks, parity, routes_ref, *refs):
    row_refs, refs = refs[:blocks], refs[blocks:]
    before_refs, (keep_ref, send_ref, rows, sems) = refs[:-4], refs[-4:]
    size = row_refs[0].shape[0]
    if before_refs:
        for i in range(blocks):
            rows[i * size : (i + 1) * size, :] = row_refs[i][...]
    else:
        fetch([(row_refs[i], rows.at[pl.ds(i * size, size), :]) for i in range(blocks)], sems)
    tokens = routes_ref.shape[0] // 2
    lane = lax.broadcasted_iota(jnp.int32, (tokens, blocks * size), 1)
    slots = (lane + (lax.div(lane, size) + parity) * size).astype(jnp.float32)
    for i, out_ref in enumerate((keep_ref, send_ref)):
        part = slice(i * tokens, (i + 1) * tokens)
        first = routes_ref[part, 0:1]
        total = before_refs[i][...] if before_refs else None
        for j, weight in enumerate((first, 1.0 - first)):
            pick = (slots == routes_ref[part, j + 1 : j + 2]).astype(jnp.float32).astype(jnp.bfloat16)
            term = weight * jnp.dot(pick, rows[...], preferred_element_type=jnp.float32)
            total = term if total is None else total + term
        out_ref[...] = total.astype(out_ref.dtype)


def combine(row_blocks, parity, routes, before, send_type):
    blocks = len(row_blocks)
    size, width = row_blocks[0].shape
    tokens = routes.shape[0] // 2
    vmem = pl.BlockSpec(memory_space=pltpu.VMEM)
    return pl.pallas_call(
        functools.partial(combine_kernel, blocks, parity),
        in_specs=[vmem] + [vmem if before else pl.BlockSpec(memory_space=pl.ANY)] * blocks + [vmem] * len(before),
        out_specs=[vmem] * 2,
        out_shape=[
            jax.ShapeDtypeStruct((tokens, width), jnp.float32),
            jax.ShapeDtypeStruct((tokens, width), send_type),
        ],
        scratch_shapes=[
            pltpu.VMEM((blocks * size, width), jnp.bfloat16),
            pltpu.SemaphoreType.DMA((blocks,)),
        ],
        compiler_params=pltpu.CompilerParams(vmem_limit_bytes=16 * MIB),
        cost_estimate=pl.CostEstimate(
            flops=8 * tokens * blocks * size * width,
            bytes_accessed=2 * blocks * size * width,
            transcendentals=0,
        ),
        name="combine",
    )(routes, *row_blocks, *before)


def finish_kernel(
    keep_moe_ref, got_moe_ref, hidden_ref, mod_ref, final_ref, keep_ref, got_ref, guide_final_ref, latent_ref,
    guidance_ref, step_ref, out_ref
):
    def velocity(weight_ref, values):
        return lax.dot_general(
            weight_ref[...],
            layer_norm(values).astype(jnp.bfloat16),
            (((1,), (1,)), ((), ())),
            preferred_element_type=jnp.float32,
        )

    moe_out = keep_moe_ref[...] + got_moe_ref[...].astype(jnp.float32)
    main_velocity = velocity(final_ref, hidden_ref[0].astype(jnp.float32) + mod_ref[2] * moe_out)
    guide_velocity = velocity(guide_final_ref, keep_ref[...] + got_ref[...].astype(jnp.float32))
    guided = guide_velocity + guidance_ref[0] * (main_velocity - guide_velocity)
    out_ref[0] = latent_ref[0] + step_ref[0] * guided


def finish(keep_moe, got_moe, hidden, modulation, main_final, keep, got, guide_final, latent, guidance, step_size):
    vmem = pl.BlockSpec(memory_space=pltpu.VMEM)
    smem = pl.BlockSpec(memory_space=pltpu.SMEM)
    return pl.pallas_call(
        finish_kernel,
        in_specs=[vmem] * 9 + [smem] * 2,
        out_specs=vmem,
        out_shape=jax.ShapeDtypeStruct(latent.shape, latent.dtype),
        compiler_params=pltpu.CompilerParams(vmem_limit_bytes=16 * MIB),
        cost_estimate=pl.CostEstimate(flops=hidden.size * 64, bytes_accessed=hidden.size * 8, transcendentals=0),
        name="finish",
    )(keep_moe, got_moe, hidden, modulation, main_final, keep, got, guide_final, latent, guidance, step_size)


def direct_body(*args):
    return direct_step(*args)


def direct_step(
    hidden, modulation, router_weight, route_ids, gate_weight, up_weight, down_weight, main_final, guide_qkv,
    guide_out, guide_final, latent, guidance, step_size,
):
    tokens = hidden.shape[1]
    devices = lax.axis_size(MEMBERS)
    capacity = max(2, 2 * tokens * TOP // EXPERTS)
    me = lax.axis_index(MEMBERS).astype(jnp.int32)[None]
    head = lax.axis_index("head").astype(jnp.int32)[None]

    def swap(block, k):
        if k == 0:
            return block
        return lax.ppermute(block, MEMBERS, [(i, i ^ k) for i in range(devices)])

    modulation = jnp.transpose(modulation, (1, 0, 2))
    ids = jnp.transpose(route_ids, (0, 2, 1))
    other = swap(hidden, 1)
    other_ids = swap(ids, 1)
    rows = own_rows(hidden, modulation)
    rows, code, *outgoing = prep(me, ids, other_ids, rows, other, modulation, devices // 2, capacity)
    rows_a = [swap(outgoing[k // 2], k) for k in CHUNK_A]
    rows_b = [swap(outgoing[k // 2], k) for k in CHUNK_B]
    queries, kv, routes = side(
        rows, router_weight.T, ids, other_ids, code, jnp.transpose(guide_qkv[0], (1, 2, 0))
    )
    weights, _ = lax.optimization_barrier(((gate_weight, up_weight, down_weight), routes))
    kept = resident(*weights)
    far = swap(kv, 8)
    near = swap(kv, 4)
    rows_a, routes, queries = lax.optimization_barrier((rows_a, routes, queries))

    done_a = ffn(rows_a, kept, gate_weight, up_weight, down_weight)
    back_a = [swap(block, k) for block, k in zip(done_a, CHUNK_A)]

    done_b = ffn(rows_b, kept, gate_weight, up_weight, down_weight)
    done_b, queries, back_a, far, near = lax.optimization_barrier((done_b, queries, back_a, far, near))
    back_b = [swap(block, k) for block, k in zip(done_b, CHUNK_B)]
    relayed = swap(far, 4)

    keep, send = attend(head, queries, [kv, near, far, relayed], guide_out)
    got = swap(send, 1)
    sums = combine([block for _, block in sorted(zip(CHUNK_A, back_a), key=lambda pair: pair[0])], 0, routes, (), jnp.float32)
    keep_moe, send_moe = combine(
        [block for _, block in sorted(zip(CHUNK_B, back_b), key=lambda pair: pair[0])], 1, routes, sums, jnp.bfloat16
    )
    got_moe = swap(send_moe, 1)
    result = finish(
        keep_moe, got_moe, hidden, modulation, main_final.T, keep, got, guide_final.T,
        jnp.transpose(latent, (0, 2, 1)), guidance, step_size,
    )
    return jnp.transpose(result, (0, 2, 1))


def route_slots(flat_ids, block_slots, per_index, copies):
    route_flat = flat_ids.reshape(-1)
    one_hot = (route_flat[:, None] == jnp.arange(EXPERTS, dtype=jnp.int32)[None, :]).astype(
        jnp.int32
    )
    earlier = jnp.cumsum(one_hot, axis=0) - one_hot
    earlier_count = jnp.sum(earlier * one_hot, axis=1)
    slot_pos = route_flat % per_index * block_slots + earlier_count
    targets = (
        route_flat[:, None] * copies + jnp.arange(copies, dtype=jnp.int32)[None, :]
    ) // per_index
    return (targets, slot_pos)


def expert_hidden(
    rows, positions, gate_weight, up_weight, my_expert, index_first, block_slots, copies
):
    owner_expert = (index_first + positions // block_slots) // copies
    keep_mask = (owner_expert == my_expert).astype(jnp.float32)[:, None]
    gate_vals = jnp.dot(rows, gate_weight, preferred_element_type=jnp.float32)
    up_vals = jnp.dot(rows, up_weight, preferred_element_type=jnp.float32)
    return (jax.nn.silu(gate_vals) * up_vals * keep_mask).astype(jnp.bfloat16)


def spread_body(
    hidden,
    modulation,
    router_weight,
    route_ids,
    gate_weight,
    up_weight,
    down_weight,
    main_final,
    guide_qkv,
    guide_out,
    guide_final,
    latent,
    guidance,
    step_size,
):
    lat_dev, tok_dev, width = hidden.shape
    experts_axis = lax.axis_size("expert")
    group_size = lax.axis_size(("dp", "head"))
    slice_units = gate_weight.shape[1]
    index_units = slice_units * group_size
    if EXPERTS >= experts_axis:
        per_index = EXPERTS // experts_axis
        copies = 1
    else:
        per_index = 1
        copies = experts_axis // EXPERTS
    capacity = max(2, 2 * tok_dev * TOP // EXPERTS)
    block_slots = lat_dev * capacity
    slot_count = per_index * block_slots
    my_index = lax.axis_index("expert")
    my_member = lax.axis_index(("dp", "head"))
    my_expert = (my_index * index_units + my_member * slice_units) // FF
    index_first = my_index * per_index
    hidden_float = hidden.astype(jnp.float32)
    modulated = (
        layer_norm(hidden_float) * (1.0 + modulation[:, 1][:, None, :])
        + modulation[:, 0][:, None, :]
    ).astype(jnp.bfloat16)
    row_count = lat_dev * tok_dev
    flat_rows = modulated.reshape(row_count, width)
    logits = jnp.dot(flat_rows.astype(jnp.float32), router_weight, precision=lax.Precision.HIGHEST)
    flat_ids = route_ids.reshape(row_count, TOP)
    picked = jnp.take_along_axis(logits, flat_ids, axis=1)
    first_weight = jax.nn.sigmoid(picked[:, 0] - picked[:, 1])
    route_weight = jnp.stack([first_weight, 1.0 - first_weight], axis=1)
    route_count = row_count * TOP
    route_token = jnp.arange(route_count, dtype=jnp.int32) // TOP
    targets, slot_pos = route_slots(flat_ids, block_slots, per_index, copies)
    outgoing = jnp.zeros((experts_axis, slot_count, width), jnp.bfloat16)
    payload = jnp.broadcast_to(flat_rows[route_token][:, None, :], (route_count, copies, width))
    outgoing = outgoing.at[targets, slot_pos[:, None]].set(payload)
    received = lax.all_to_all(outgoing, "expert", split_axis=0, concat_axis=0, tiled=True)
    received_rows = received.reshape(experts_axis * slot_count, width)
    piece = lax.all_gather(received_rows, ("dp", "head"), axis=0, tiled=True)
    positions = jnp.arange(piece.shape[0], dtype=jnp.int32) % slot_count
    activated = expert_hidden(
        piece, positions, gate_weight, up_weight, my_expert, index_first, block_slots, copies
    )
    term = jnp.dot(activated, down_weight, preferred_element_type=jnp.float32)
    row_sums = lax.psum_scatter(
        lax.optimization_barrier(term.astype(jnp.bfloat16))
        .astype(jnp.float32)
        .astype(jnp.bfloat16),
        ("dp", "head"),
        scatter_dimension=0,
        tiled=True,
    ).astype(jnp.float32)
    returned = lax.all_to_all(
        row_sums.reshape(experts_axis, slot_count, width).astype(jnp.bfloat16),
        "expert",
        split_axis=0,
        concat_axis=0,
        tiled=True,
    ).astype(jnp.float32)
    gathered_back = returned[targets, slot_pos[:, None]]
    per_route = jnp.sum(gathered_back, axis=1).reshape(row_count, TOP, width)
    moe_out = jnp.sum(per_route * route_weight[:, :, None], axis=1)
    updated = hidden_float + modulation[:, 2][:, None, :] * moe_out.reshape(lat_dev, tok_dev, width)
    main_norm = layer_norm(updated).astype(jnp.bfloat16)
    main_velocity = jnp.dot(
        main_norm.reshape(row_count, width), main_final, preferred_element_type=jnp.float32
    ).reshape(lat_dev, tok_dev, P_SIZE)
    queries = unit_rows(guide_qkv[..., :HD].astype(jnp.float32)).astype(jnp.bfloat16)
    unit_keys = unit_rows(guide_qkv[..., HD : 2 * HD].astype(jnp.float32)).astype(jnp.bfloat16)
    key_value = jnp.concatenate([unit_keys, guide_qkv[..., 2 * HD :]], axis=-1)
    piece = lax.all_gather(key_value, "expert", axis=1, tiled=True)
    key_piece = piece[..., :HD]
    value_piece = piece[..., HD:]
    scores = jnp.einsum(
        "lqhc,lkhc->lhqk", queries, key_piece, preferred_element_type=jnp.float32
    ) * (score_scale / HD)
    weights = jnp.exp(scores - score_scale)
    weighted_sum = jnp.einsum(
        "lhqk,lkhc->lqhc",
        weights.astype(jnp.bfloat16),
        value_piece,
        preferred_element_type=jnp.float32,
    )
    weight_total = jnp.transpose(jnp.sum(weights, axis=-1), (0, 2, 1))
    attended = (weighted_sum / weight_total[..., None]).astype(jnp.bfloat16)
    partial_mix = jnp.einsum(
        "lqhc,hcd->lqd", attended, guide_out, preferred_element_type=jnp.float32
    )
    guide_mix = lax.psum_scatter(
        partial_mix.astype(jnp.bfloat16), "head", scatter_dimension=1, tiled=True
    ).astype(jnp.float32)
    guide_norm = layer_norm(guide_mix).astype(jnp.bfloat16)
    guide_width = guide_norm.shape[-1]
    guide_velocity = jnp.dot(
        guide_norm.reshape(row_count, guide_width), guide_final, preferred_element_type=jnp.float32
    ).reshape(lat_dev, tok_dev, P_SIZE)
    guided = guide_velocity + guidance[:, None, None] * (main_velocity - guide_velocity)
    return latent + step_size[:, None, None] * guided


def solution(mesh):
    in_specs = (
        P(("groups", "dp"), ("expert", "head"), None),
        P(("groups", "dp"), None, None),
        P(),
        P(("groups", "dp"), ("expert", "head"), None),
        P(None, ("expert", "dp", "head")),
        P(None, ("expert", "dp", "head")),
        P(("expert", "dp", "head"), None),
        P(),
        P(("groups", "dp"), "expert", "head", None),
        P("head", None, None),
        P(),
        P(("groups", "dp"), ("expert", "head"), None),
        P(("groups", "dp")),
        P(("groups", "dp")),
    )
    out_specs = P(("groups", "dp"), ("expert", "head"), None)
    sizes = dict(mesh.shape)
    members = sizes["expert"] * sizes["dp"] * sizes["head"]
    direct = members == EXPERTS and sizes["expert"] == 4 and sizes["head"] == 2
    body = direct_body if direct else spread_body
    return jax.shard_map(body, mesh=mesh, in_specs=in_specs, out_specs=out_specs, check_vma=False)
```

```python
import functools

import jax
import jax.numpy as jnp
from jax import lax
from jax.experimental import pallas as pl
from jax.experimental.pallas import tpu as pltpu
from jax.sharding import PartitionSpec as P


FF = 6144
EXPERTS = 16
TOP = 2
HD = 64
P_SIZE = 16


epsilon = 1e-06
score_scale = 8.0
MIB = 1024 * 1024
MEMBERS = ("expert", "dp", "head")
CHUNK_A = [8, 12, 4, 2]
CHUNK_B = [6, 10, 14, 0]


def layer_norm(values):
    average = jnp.mean(values, axis=-1, keepdims=True)
    centered = values - average
    return centered / jnp.sqrt(jnp.mean(centered * centered, axis=-1, keepdims=True) + epsilon)


def unit_rows(values):
    return values / jnp.sqrt(jnp.mean(values * values, axis=-1, keepdims=True) + epsilon)


def modulate(values, mod_ref):
    return (layer_norm(values.astype(jnp.float32)) * (1.0 + mod_ref[1]) + mod_ref[0]).astype(jnp.bfloat16)


def fetch(pairs, sems):
    copies = [pltpu.make_async_copy(src, dst, sems.at[i]) for i, (src, dst) in enumerate(pairs)]
    for copy in copies:
        copy.start()
    for copy in copies:
        copy.wait()


def own_rows_kernel(own_hbm, mod_hbm, ids_hbm, rows_ref, mod_ref, ids_ref, own, sems):
    fetch([(own_hbm, own), (mod_hbm, mod_ref), (ids_hbm, ids_ref)], sems)
    rows_ref[...] = modulate(own[0], mod_ref)


def own_rows(own, modulation, ids):
    hbm, vmem = pl.BlockSpec(memory_space=pltpu.HBM), pl.BlockSpec(memory_space=pltpu.VMEM)
    return pl.pallas_call(
        own_rows_kernel,
        in_specs=[hbm] * 3,
        out_specs=[vmem] * 3,
        out_shape=[
            jax.ShapeDtypeStruct(own.shape[1:], jnp.bfloat16),
            jax.ShapeDtypeStruct(modulation.shape, modulation.dtype),
            jax.ShapeDtypeStruct(ids.shape, ids.dtype),
        ],
        scratch_shapes=[pltpu.VMEM(own.shape, own.dtype), pltpu.SemaphoreType.DMA((3,))],
        compiler_params=pltpu.CompilerParams(vmem_limit_bytes=16 * MIB),
        cost_estimate=pl.CostEstimate(flops=8 * own.size, bytes_accessed=4 * own.size, transcendentals=0),
        name="own_rows",
    )(own, modulation, ids)


def prep_kernel(
    chips, capacity, me_ref, own_ids, other_ids, own_rows_ref, other, mod, rows_ref, code_ref, *out_refs
):
    tokens = own_rows_ref.shape[0]
    both = 2 * tokens
    rows_ref[:tokens, :] = own_rows_ref[...]
    rows_ref[tokens:, :] = modulate(other[0], mod)
    me = me_ref[0]
    ids = jnp.concatenate([own_ids[0], other_ids[0]], axis=1)
    experts = lax.broadcasted_iota(jnp.int32, (EXPERTS, both), 0)
    named = [experts == ids[j : j + 1, :] for j in range(TOP)]
    tally = functools.reduce(jnp.logical_or, named).astype(jnp.float32).astype(jnp.bfloat16)
    earlier = lax.broadcasted_iota(jnp.int32, (both, both), 0)
    later = lax.broadcasted_iota(jnp.int32, (both, both), 1)
    before = jnp.logical_and(earlier < later, jnp.logical_or(later < tokens, earlier >= tokens))
    rank = jnp.dot(
        tally, before.astype(jnp.float32).astype(jnp.bfloat16), preferred_element_type=jnp.float32
    )
    second = jnp.where(lax.broadcasted_iota(jnp.int32, (1, both), 1) >= tokens, capacity, 0)
    slots = lax.broadcasted_iota(jnp.int32, (2 * chips * capacity, both), 0)
    hit = None
    for j in range(TOP):
        own_rank = jnp.sum(jnp.where(named[j], rank, 0.0), axis=0, keepdims=True).astype(jnp.int32)
        away = jnp.bitwise_xor(ids[j : j + 1, :], me)
        code = lax.shift_right_logical(away, 1) * (2 * capacity) + second + own_rank
        code = jnp.where(jnp.bitwise_and(away, 1) == 0, code, -1)
        code_ref[j : j + 1, :] = code
        hit = slots == code if hit is None else jnp.logical_or(hit, slots == code)
    select = hit.astype(jnp.float32).astype(jnp.bfloat16)
    for p, out_ref in enumerate(out_refs):
        out_ref[...] = jnp.dot(
            select[2 * p * capacity : 2 * (p + 1) * capacity, :],
            rows_ref[...],
            preferred_element_type=jnp.float32,
        ).astype(jnp.bfloat16)


def prep(me, own_ids, other_ids, rows, other, modulation, chips, capacity):
    tokens, width = rows.shape
    vmem = pl.BlockSpec(memory_space=pltpu.VMEM)
    return pl.pallas_call(
        functools.partial(prep_kernel, chips, capacity),
        in_specs=[pl.BlockSpec(memory_space=pltpu.SMEM)] + [vmem] * 5,
        out_specs=[vmem] * (2 + chips),
        out_shape=[
            jax.ShapeDtypeStruct((2 * tokens, width), jnp.bfloat16),
            jax.ShapeDtypeStruct((TOP, 2 * tokens), jnp.int32),
        ]
        + [jax.ShapeDtypeStruct((2 * capacity, width), jnp.bfloat16)] * chips,
        compiler_params=pltpu.CompilerParams(vmem_limit_bytes=16 * MIB),
        cost_estimate=pl.CostEstimate(
            flops=8 * chips * capacity * tokens * width,
            bytes_accessed=4 * chips * capacity * width,
            transcendentals=0,
        ),
        name="prep",
    )(me, own_ids, other_ids, rows, other, modulation)


RESIDENT = 1


def weight_tile(units):
    return 768 if units % 768 == 0 else 128


def resident_kernel(gate_hbm, up_hbm, down_hbm, gate_ref, up_ref, down_ref, sems):
    part = pl.ds(0, gate_ref.shape[1])
    fetch(
        [(gate_hbm.at[:, part], gate_ref), (up_hbm.at[:, part], up_ref), (down_hbm.at[part, :], down_ref)], sems
    )


def resident(gate_weight, up_weight, down_weight):
    width, units = gate_weight.shape
    kept = RESIDENT * weight_tile(units)
    vmem, hbm = pl.BlockSpec(memory_space=pltpu.VMEM), pl.BlockSpec(memory_space=pltpu.HBM)
    return pl.pallas_call(
        resident_kernel,
        in_specs=[hbm] * 3,
        out_specs=[vmem] * 3,
        out_shape=[
            jax.ShapeDtypeStruct((width, kept), jnp.bfloat16),
            jax.ShapeDtypeStruct((width, kept), jnp.bfloat16),
            jax.ShapeDtypeStruct((kept, width), jnp.bfloat16),
        ],
        scratch_shapes=[pltpu.SemaphoreType.DMA((3,))],
        compiler_params=pltpu.CompilerParams(vmem_limit_bytes=46 * MIB),
        cost_estimate=pl.CostEstimate(flops=0, bytes_accessed=6 * width * kept, transcendentals=0),
        name="resident",
    )(gate_weight, up_weight, down_weight)


def ffn_kernel(blocks, tiles, *refs):
    row_refs = refs[:blocks]
    kept_gate, kept_up, kept_down, gate_hbm, up_hbm, down_hbm = refs[blocks : blocks + 6]
    out_refs = refs[blocks + 6 : 2 * blocks + 6]
    rows, total, hidden, gate, up, down, sems = refs[2 * blocks + 6 :]
    size = row_refs[0].shape[0]
    slots, tile = down.shape[0], down.shape[1]

    def copies(step):
        slot, part = lax.rem(step, slots), pl.ds(pl.multiple_of(step * tile, tile), tile)
        return (
            pltpu.make_async_copy(gate_hbm.at[:, part], gate.at[slot], sems.at[0, slot]),
            pltpu.make_async_copy(up_hbm.at[:, part], up.at[slot], sems.at[1, slot]),
            pltpu.make_async_copy(down_hbm.at[part, :], down.at[slot], sems.at[2, slot]),
        )

    def start(step):
        for copy in copies(step):
            copy.start()

    def units_of(gate_tile, up_tile):
        gate_vals = jnp.dot(rows[...], gate_tile, preferred_element_type=jnp.float32)
        up_vals = jnp.dot(rows[...], up_tile, preferred_element_type=jnp.float32)
        return gate_vals, up_vals

    def activate(gate_vals, up_vals):
        return (gate_vals / (1.0 + jnp.exp(-gate_vals)) * up_vals).astype(jnp.bfloat16)

    def part_of(step):
        return slice(step * tile, (step + 1) * tile)

    for step in range(RESIDENT, min(RESIDENT + slots, tiles)):
        start(jnp.int32(step))
    for i in range(blocks):
        rows[i * size : (i + 1) * size, :] = row_refs[i][...]
    hidden[0] = activate(*units_of(kept_gate[:, part_of(0)], kept_up[:, part_of(0)]))

    for step in range(1, RESIDENT):
        vals = units_of(kept_gate[:, part_of(step)], kept_up[:, part_of(step)])
        term = jnp.dot(hidden[(step - 1) % 2], kept_down[part_of(step - 1), :], preferred_element_type=jnp.float32)
        total[...] = term if step == 1 else total[...] + term
        hidden[step % 2] = activate(*vals)

    def wait_units(step):
        gate_copy, up_copy, _ = copies(step)
        gate_copy.wait()
        up_copy.wait()

    wait_units(jnp.int32(RESIDENT))
    vals = units_of(gate[RESIDENT % slots], up[RESIDENT % slots])
    term = jnp.dot(
        hidden[(RESIDENT - 1) % 2], kept_down[part_of(RESIDENT - 1), :], preferred_element_type=jnp.float32
    )
    total[...] = term if RESIDENT == 1 else total[...] + term
    hidden[RESIDENT % 2] = activate(*vals)

    def body(step, carry):
        slot, last = lax.rem(step, slots), lax.rem(step - 1, slots)
        wait_units(step)
        copies(step - 1)[2].wait()
        now = lax.rem(step, 2)
        vals = units_of(gate[slot], up[slot])
        total[...] += jnp.dot(hidden[1 - now], down[last], preferred_element_type=jnp.float32)
        hidden[now] = activate(*vals)

        @pl.when(step + slots - 1 < tiles)
        def _():
            start(step + slots - 1)

        return carry

    lax.fori_loop(RESIDENT + 1, tiles, body, 0)
    copies(jnp.int32(tiles - 1))[2].wait()
    done = total[...] + jnp.dot(
        hidden[(tiles - 1) % 2], down[(tiles - 1) % slots], preferred_element_type=jnp.float32
    )
    for i in range(blocks):
        out_refs[i][...] = done[i * size : (i + 1) * size, :].astype(jnp.bfloat16)


def ffn(row_blocks, kept, gate_weight, up_weight, down_weight):
    blocks = len(row_blocks)
    size, width = row_blocks[0].shape
    units = gate_weight.shape[1]
    tile = weight_tile(units)
    rows, slots = blocks * size, 3
    vmem, hbm = pl.BlockSpec(memory_space=pltpu.VMEM), pl.BlockSpec(memory_space=pltpu.HBM)
    return pl.pallas_call(
        functools.partial(ffn_kernel, blocks, units // tile),
        in_specs=[vmem] * (blocks + 3) + [hbm] * 3,
        out_specs=[vmem] * blocks,
        out_shape=[jax.ShapeDtypeStruct((size, width), jnp.bfloat16)] * blocks,
        scratch_shapes=[
            pltpu.VMEM((rows, width), jnp.bfloat16),
            pltpu.VMEM((rows, width), jnp.float32),
            pltpu.VMEM((2, rows, tile), jnp.bfloat16),
            pltpu.VMEM((slots, width, tile), jnp.bfloat16),
            pltpu.VMEM((slots, width, tile), jnp.bfloat16),
            pltpu.VMEM((slots, tile, width), jnp.bfloat16),
            pltpu.SemaphoreType.DMA((3, slots)),
        ],
        compiler_params=pltpu.CompilerParams(vmem_limit_bytes=36 * MIB),
        cost_estimate=pl.CostEstimate(
            flops=6 * rows * width * units,
            bytes_accessed=6 * width * units,
            transcendentals=rows * units,
        ),
        name="ffn",
    )(*row_blocks, *kept, gate_weight, up_weight, down_weight)


def side_kernel(
    rows_ref, router_hbm, own_ids_ref, other_ids_ref, code_ref, qkv_hbm, q_ref, kv_ref, routes_ref, router_ref,
    qkv, sems
):
    copy = pltpu.make_async_copy(qkv_hbm, qkv, sems.at[1])
    copy.start()
    fetch([(router_hbm, router_ref)], sems)
    logits = lax.dot_general(
        router_ref[...],
        rows_ref[...].astype(jnp.float32),
        (((1,), (1,)), ((), ())),
        precision=lax.Precision.HIGHEST,
        preferred_element_type=jnp.float32,
    )
    ids = jnp.concatenate([own_ids_ref[0], other_ids_ref[0]], axis=1)
    experts = lax.broadcasted_iota(jnp.int32, logits.shape, 0)
    picked = [
        jnp.sum(jnp.where(experts == ids[j : j + 1, :], logits, 0.0), axis=0, keepdims=True)
        for j in range(TOP)
    ]
    first = 1.0 / (1.0 + jnp.exp(picked[1] - picked[0]))
    line = lax.broadcasted_iota(jnp.int32, (8, first.shape[1]), 0)
    table = jnp.where(line == 0, first, 0.0)
    for j in range(TOP):
        table = jnp.where(line == j + 1, code_ref[j : j + 1, :].astype(jnp.float32), table)
    routes_ref[...] = jnp.transpose(table)

    def unit(values):
        return (
            values / jnp.sqrt(jnp.mean(values * values, axis=0, keepdims=True) + epsilon)
        ).astype(jnp.bfloat16)

    copy.wait()
    for h in range(qkv.shape[0]):
        q_ref[h] = unit(qkv[h, :HD, :].astype(jnp.float32))
        kv_ref[h, :HD, :] = unit(qkv[h, HD : 2 * HD, :].astype(jnp.float32))
        kv_ref[h, HD:, :] = qkv[h, 2 * HD :, :]


def side(rows, router, own_ids, other_ids, code, qkv):
    heads, _, tokens = qkv.shape
    vmem, hbm = pl.BlockSpec(memory_space=pltpu.VMEM), pl.BlockSpec(memory_space=pltpu.HBM)
    return pl.pallas_call(
        side_kernel,
        in_specs=[vmem, hbm, vmem, vmem, vmem, hbm],
        out_specs=[vmem] * 3,
        out_shape=[
            jax.ShapeDtypeStruct((heads, HD, tokens), jnp.bfloat16),
            jax.ShapeDtypeStruct((heads, 2 * HD, tokens), jnp.bfloat16),
            jax.ShapeDtypeStruct((rows.shape[0], 8), jnp.float32),
        ],
        scratch_shapes=[
            pltpu.VMEM(router.shape, router.dtype),
            pltpu.VMEM(qkv.shape, qkv.dtype),
            pltpu.SemaphoreType.DMA((2,)),
        ],
        compiler_params=pltpu.CompilerParams(vmem_limit_bytes=16 * MIB),
        cost_estimate=pl.CostEstimate(
            flops=6 * qkv.size + 12 * rows.size * EXPERTS, bytes_accessed=4 * qkv.size, transcendentals=0
        ),
        name="side",
    )(rows, router, own_ids, other_ids, code, qkv)


def attend_kernel(pieces, head_ref, q_ref, *refs):
    kv_refs = refs[:pieces]
    out_ref, keep_ref, send_ref, mix = refs[pieces:]
    heads, _, queries = q_ref.shape
    for h in range(heads):
        sums, weighted = None, None
        for kv_ref in kv_refs:
            scores = lax.dot_general(
                kv_ref[h, :HD, :], q_ref[h], (((0,), (0,)), ((), ())), preferred_element_type=jnp.float32
            ) * (score_scale / HD)
            weights = jnp.exp(scores - score_scale)
            part = jnp.sum(weights, axis=0, keepdims=True)
            value = jnp.dot(
                kv_ref[h, HD:, :], weights.astype(jnp.bfloat16), preferred_element_type=jnp.float32
            )
            sums = part if sums is None else sums + part
            weighted = value if weighted is None else weighted + value
        attended = (weighted / sums).astype(jnp.bfloat16)
        term = lax.dot_general(
            attended, out_ref[h], (((0,), (0,)), ((), ())), preferred_element_type=jnp.float32
        )
        if h == 0:
            mix[...] = term
        else:
            mix[...] += term
    half = queries // 2
    mine = head_ref[0]
    keep_ref[...] = mix[pl.ds(pl.multiple_of(mine * half, half), half), :]
    send_ref[...] = mix[pl.ds(pl.multiple_of((1 - mine) * half, half), half), :].astype(jnp.bfloat16)


def attend(head, queries, kv_pieces, guide_out):
    heads, _, count = queries.shape
    keys = sum(piece.shape[2] for piece in kv_pieces)
    wide = guide_out.shape[-1]
    vmem = pl.BlockSpec(memory_space=pltpu.VMEM)
    return pl.pallas_call(
        functools.partial(attend_kernel, len(kv_pieces)),
        in_specs=[pl.BlockSpec(memory_space=pltpu.SMEM)] + [vmem] * (2 + len(kv_pieces)),
        out_specs=[vmem, vmem],
        out_shape=[
            jax.ShapeDtypeStruct((count // 2, wide), jnp.float32),
            jax.ShapeDtypeStruct((count // 2, wide), jnp.bfloat16),
        ],
        scratch_shapes=[pltpu.VMEM((count, wide), jnp.float32)],
        compiler_params=pltpu.CompilerParams(vmem_limit_bytes=16 * MIB),
        cost_estimate=pl.CostEstimate(
            flops=4 * heads * count * keys * HD,
            bytes_accessed=4 * heads * keys * HD,
            transcendentals=heads * count * keys,
        ),
        name="attend",
    )(head, queries, *kv_pieces, guide_out)


def combine_kernel(chips, routes_ref, *refs):
    blocks = len(chips)
    row_refs, refs = refs[:blocks], refs[blocks:]
    before_refs, (keep_ref, send_ref, rows, sems) = refs[:-4], refs[-4:]
    size = row_refs[0].shape[0]
    if before_refs:
        for i in range(blocks):
            rows[i * size : (i + 1) * size, :] = row_refs[i][...]
    else:
        fetch([(row_refs[i], rows.at[pl.ds(i * size, size), :]) for i in range(blocks)], sems)
    tokens = routes_ref.shape[0] // 2
    lane = lax.broadcasted_iota(jnp.int32, (tokens, blocks * size), 1)
    slots = lane
    for i, chip in enumerate(chips):
        inside = jnp.logical_and(lane >= i * size, lane < (i + 1) * size)
        slots = jnp.where(inside, lane + (chip - i) * size, slots)
    slots = slots.astype(jnp.float32)
    for i, out_ref in enumerate((keep_ref, send_ref)):
        part = slice(i * tokens, (i + 1) * tokens)
        first = routes_ref[part, 0:1]
        total = before_refs[i][...] if before_refs else None
        for j, weight in enumerate((first, 1.0 - first)):
            pick = (slots == routes_ref[part, j + 1 : j + 2]).astype(jnp.float32).astype(jnp.bfloat16)
            term = weight * jnp.dot(pick, rows[...], preferred_element_type=jnp.float32)
            total = term if total is None else total + term
        out_ref[...] = total.astype(out_ref.dtype)


def combine(row_blocks, chips, routes, before, send_type):
    blocks = len(row_blocks)
    size, width = row_blocks[0].shape
    tokens = routes.shape[0] // 2
    vmem = pl.BlockSpec(memory_space=pltpu.VMEM)
    return pl.pallas_call(
        functools.partial(combine_kernel, chips),
        in_specs=[vmem] + [vmem if before else pl.BlockSpec(memory_space=pl.ANY)] * blocks + [vmem] * len(before),
        out_specs=[vmem] * 2,
        out_shape=[
            jax.ShapeDtypeStruct((tokens, width), jnp.float32),
            jax.ShapeDtypeStruct((tokens, width), send_type),
        ],
        scratch_shapes=[
            pltpu.VMEM((blocks * size, width), jnp.bfloat16),
            pltpu.SemaphoreType.DMA((blocks,)),
        ],
        compiler_params=pltpu.CompilerParams(vmem_limit_bytes=16 * MIB),
        cost_estimate=pl.CostEstimate(
            flops=8 * tokens * blocks * size * width,
            bytes_accessed=2 * blocks * size * width,
            transcendentals=0,
        ),
        name="combine",
    )(routes, *row_blocks, *before)


def finish_kernel(
    keep_moe_ref, got_moe_ref, hidden_ref, mod_ref, final_ref, keep_ref, got_ref, guide_final_ref, latent_ref,
    guidance_ref, step_ref, out_ref
):
    def velocity(weight_ref, values):
        return lax.dot_general(
            weight_ref[...],
            layer_norm(values).astype(jnp.bfloat16),
            (((1,), (1,)), ((), ())),
            preferred_element_type=jnp.float32,
        )

    moe_out = keep_moe_ref[...] + got_moe_ref[...].astype(jnp.float32)
    main_velocity = velocity(final_ref, hidden_ref[0].astype(jnp.float32) + mod_ref[2] * moe_out)
    guide_velocity = velocity(guide_final_ref, keep_ref[...] + got_ref[...].astype(jnp.float32))
    guided = guide_velocity + guidance_ref[0] * (main_velocity - guide_velocity)
    out_ref[0] = latent_ref[0] + step_ref[0] * guided


def finish(keep_moe, got_moe, hidden, modulation, main_final, keep, got, guide_final, latent, guidance, step_size):
    vmem = pl.BlockSpec(memory_space=pltpu.VMEM)
    smem = pl.BlockSpec(memory_space=pltpu.SMEM)
    return pl.pallas_call(
        finish_kernel,
        in_specs=[vmem] * 9 + [smem] * 2,
        out_specs=vmem,
        out_shape=jax.ShapeDtypeStruct(latent.shape, latent.dtype),
        compiler_params=pltpu.CompilerParams(vmem_limit_bytes=16 * MIB),
        cost_estimate=pl.CostEstimate(flops=hidden.size * 64, bytes_accessed=hidden.size * 8, transcendentals=0),
        name="finish",
    )(keep_moe, got_moe, hidden, modulation, main_final, keep, got, guide_final, latent, guidance, step_size)


def direct_body(*args):
    return direct_step(*args)


def direct_step(
    hidden, modulation, router_weight, route_ids, gate_weight, up_weight, down_weight, main_final, guide_qkv,
    guide_out, guide_final, latent, guidance, step_size,
):
    tokens = hidden.shape[1]
    devices = lax.axis_size(MEMBERS)
    capacity = max(2, 2 * tokens * TOP // EXPERTS)
    me = lax.axis_index(MEMBERS).astype(jnp.int32)[None]
    head = lax.axis_index("head").astype(jnp.int32)[None]

    def swap(block, k):
        if k == 0:
            return block
        return lax.ppermute(block, MEMBERS, [(i, i ^ k) for i in range(devices)])

    modulation = jnp.transpose(modulation, (1, 0, 2))
    ids = jnp.transpose(route_ids, (0, 2, 1))
    other = swap(hidden, 1)
    other_ids = swap(ids, 1)
    rows, near_modulation, near_ids = own_rows(hidden, modulation, ids)
    rows, code, *outgoing = prep(
        me, near_ids, other_ids, rows, other, near_modulation, devices // 2, capacity
    )
    rows_a = [swap(outgoing[k // 2], k) for k in CHUNK_A]
    rows_b = [swap(outgoing[k // 2], k) for k in CHUNK_B]
    queries, kv, routes = side(rows, router_weight.T, near_ids, other_ids, code, jnp.transpose(guide_qkv[0], (1, 2, 0)))
    weights, _ = lax.optimization_barrier(((gate_weight, up_weight, down_weight), routes))
    kept = resident(*weights)
    far = swap(kv, 8)
    near = swap(kv, 4)
    rows_a, routes, queries = lax.optimization_barrier((rows_a, routes, queries))

    done_a = ffn(rows_a, kept, gate_weight, up_weight, down_weight)
    back_a = [swap(block, k) for block, k in zip(done_a, CHUNK_A)]

    done_b = ffn(rows_b, kept, gate_weight, up_weight, down_weight)
    done_b, queries, back_a, far, near = lax.optimization_barrier((done_b, queries, back_a, far, near))
    back_b = [swap(block, k) for block, k in zip(done_b, CHUNK_B)]
    relayed = swap(far, 4)

    keep, send = attend(head, queries, [kv, near, far, relayed], guide_out)
    got = swap(send, 1)
    sums = combine(back_a, [k // 2 for k in CHUNK_A], routes, (), jnp.float32)
    keep_moe, send_moe = combine(back_b, [k // 2 for k in CHUNK_B], routes, sums, jnp.bfloat16)
    got_moe = swap(send_moe, 1)
    result = finish(
        keep_moe, got_moe, hidden, modulation, main_final.T, keep, got, guide_final.T,
        jnp.transpose(latent, (0, 2, 1)), guidance, step_size,
    )
    return jnp.transpose(result, (0, 2, 1))


def route_slots(flat_ids, block_slots, per_index, copies):
    route_flat = flat_ids.reshape(-1)
    one_hot = (route_flat[:, None] == jnp.arange(EXPERTS, dtype=jnp.int32)[None, :]).astype(
        jnp.int32
    )
    earlier = jnp.cumsum(one_hot, axis=0) - one_hot
    earlier_count = jnp.sum(earlier * one_hot, axis=1)
    slot_pos = route_flat % per_index * block_slots + earlier_count
    targets = (
        route_flat[:, None] * copies + jnp.arange(copies, dtype=jnp.int32)[None, :]
    ) // per_index
    return (targets, slot_pos)


def expert_hidden(
    rows, positions, gate_weight, up_weight, my_expert, index_first, block_slots, copies
):
    owner_expert = (index_first + positions // block_slots) // copies
    keep_mask = (owner_expert == my_expert).astype(jnp.float32)[:, None]
    gate_vals = jnp.dot(rows, gate_weight, preferred_element_type=jnp.float32)
    up_vals = jnp.dot(rows, up_weight, preferred_element_type=jnp.float32)
    return (jax.nn.silu(gate_vals) * up_vals * keep_mask).astype(jnp.bfloat16)


def spread_body(
    hidden,
    modulation,
    router_weight,
    route_ids,
    gate_weight,
    up_weight,
    down_weight,
    main_final,
    guide_qkv,
    guide_out,
    guide_final,
    latent,
    guidance,
    step_size,
):
    lat_dev, tok_dev, width = hidden.shape
    experts_axis = lax.axis_size("expert")
    group_size = lax.axis_size(("dp", "head"))
    slice_units = gate_weight.shape[1]
    index_units = slice_units * group_size
    if EXPERTS >= experts_axis:
        per_index = EXPERTS // experts_axis
        copies = 1
    else:
        per_index = 1
        copies = experts_axis // EXPERTS
    capacity = max(2, 2 * tok_dev * TOP // EXPERTS)
    block_slots = lat_dev * capacity
    slot_count = per_index * block_slots
    my_index = lax.axis_index("expert")
    my_member = lax.axis_index(("dp", "head"))
    my_expert = (my_index * index_units + my_member * slice_units) // FF
    index_first = my_index * per_index
    hidden_float = hidden.astype(jnp.float32)
    modulated = (
        layer_norm(hidden_float) * (1.0 + modulation[:, 1][:, None, :])
        + modulation[:, 0][:, None, :]
    ).astype(jnp.bfloat16)
    row_count = lat_dev * tok_dev
    flat_rows = modulated.reshape(row_count, width)
    logits = jnp.dot(flat_rows.astype(jnp.float32), router_weight, precision=lax.Precision.HIGHEST)
    flat_ids = route_ids.reshape(row_count, TOP)
    picked = jnp.take_along_axis(logits, flat_ids, axis=1)
    first_weight = jax.nn.sigmoid(picked[:, 0] - picked[:, 1])
    route_weight = jnp.stack([first_weight, 1.0 - first_weight], axis=1)
    route_count = row_count * TOP
    route_token = jnp.arange(route_count, dtype=jnp.int32) // TOP
    targets, slot_pos = route_slots(flat_ids, block_slots, per_index, copies)
    outgoing = jnp.zeros((experts_axis, slot_count, width), jnp.bfloat16)
    payload = jnp.broadcast_to(flat_rows[route_token][:, None, :], (route_count, copies, width))
    outgoing = outgoing.at[targets, slot_pos[:, None]].set(payload)
    received = lax.all_to_all(outgoing, "expert", split_axis=0, concat_axis=0, tiled=True)
    received_rows = received.reshape(experts_axis * slot_count, width)
    piece = lax.all_gather(received_rows, ("dp", "head"), axis=0, tiled=True)
    positions = jnp.arange(piece.shape[0], dtype=jnp.int32) % slot_count
    activated = expert_hidden(
        piece, positions, gate_weight, up_weight, my_expert, index_first, block_slots, copies
    )
    term = jnp.dot(activated, down_weight, preferred_element_type=jnp.float32)
    row_sums = lax.psum_scatter(
        lax.optimization_barrier(term.astype(jnp.bfloat16))
        .astype(jnp.float32)
        .astype(jnp.bfloat16),
        ("dp", "head"),
        scatter_dimension=0,
        tiled=True,
    ).astype(jnp.float32)
    returned = lax.all_to_all(
        row_sums.reshape(experts_axis, slot_count, width).astype(jnp.bfloat16),
        "expert",
        split_axis=0,
        concat_axis=0,
        tiled=True,
    ).astype(jnp.float32)
    gathered_back = returned[targets, slot_pos[:, None]]
    per_route = jnp.sum(gathered_back, axis=1).reshape(row_count, TOP, width)
    moe_out = jnp.sum(per_route * route_weight[:, :, None], axis=1)
    updated = hidden_float + modulation[:, 2][:, None, :] * moe_out.reshape(lat_dev, tok_dev, width)
    main_norm = layer_norm(updated).astype(jnp.bfloat16)
    main_velocity = jnp.dot(
        main_norm.reshape(row_count, width), main_final, preferred_element_type=jnp.float32
    ).reshape(lat_dev, tok_dev, P_SIZE)
    queries = unit_rows(guide_qkv[..., :HD].astype(jnp.float32)).astype(jnp.bfloat16)
    unit_keys = unit_rows(guide_qkv[..., HD : 2 * HD].astype(jnp.float32)).astype(jnp.bfloat16)
    key_value = jnp.concatenate([unit_keys, guide_qkv[..., 2 * HD :]], axis=-1)
    piece = lax.all_gather(key_value, "expert", axis=1, tiled=True)
    key_piece = piece[..., :HD]
    value_piece = piece[..., HD:]
    scores = jnp.einsum(
        "lqhc,lkhc->lhqk", queries, key_piece, preferred_element_type=jnp.float32
    ) * (score_scale / HD)
    weights = jnp.exp(scores - score_scale)
    weighted_sum = jnp.einsum(
        "lhqk,lkhc->lqhc",
        weights.astype(jnp.bfloat16),
        value_piece,
        preferred_element_type=jnp.float32,
    )
    weight_total = jnp.transpose(jnp.sum(weights, axis=-1), (0, 2, 1))
    attended = (weighted_sum / weight_total[..., None]).astype(jnp.bfloat16)
    partial_mix = jnp.einsum(
        "lqhc,hcd->lqd", attended, guide_out, preferred_element_type=jnp.float32
    )
    guide_mix = lax.psum_scatter(
        partial_mix.astype(jnp.bfloat16), "head", scatter_dimension=1, tiled=True
    ).astype(jnp.float32)
    guide_norm = layer_norm(guide_mix).astype(jnp.bfloat16)
    guide_width = guide_norm.shape[-1]
    guide_velocity = jnp.dot(
        guide_norm.reshape(row_count, guide_width), guide_final, preferred_element_type=jnp.float32
    ).reshape(lat_dev, tok_dev, P_SIZE)
    guided = guide_velocity + guidance[:, None, None] * (main_velocity - guide_velocity)
    return latent + step_size[:, None, None] * guided


def solution(mesh):
    in_specs = (
        P(("groups", "dp"), ("expert", "head"), None),
        P(("groups", "dp"), None, None),
        P(),
        P(("groups", "dp"), ("expert", "head"), None),
        P(None, ("expert", "dp", "head")),
        P(None, ("expert", "dp", "head")),
        P(("expert", "dp", "head"), None),
        P(),
        P(("groups", "dp"), "expert", "head", None),
        P("head", None, None),
        P(),
        P(("groups", "dp"), ("expert", "head"), None),
        P(("groups", "dp")),
        P(("groups", "dp")),
    )
    out_specs = P(("groups", "dp"), ("expert", "head"), None)
    sizes = dict(mesh.shape)
    members = sizes["expert"] * sizes["dp"] * sizes["head"]
    direct = members == EXPERTS and sizes["expert"] == 4 and sizes["head"] == 2
    body = direct_body if direct else spread_body
    return jax.shard_map(body, mesh=mesh, in_specs=in_specs, out_specs=out_specs, check_vma=False)
```

```python
import functools

import jax
import jax.numpy as jnp
from jax import lax
from jax.experimental import pallas as pl
from jax.experimental.pallas import tpu as pltpu
from jax.sharding import PartitionSpec as P


FF = 6144
EXPERTS = 16
TOP = 2
HD = 64
P_SIZE = 16


epsilon = 1e-06
score_scale = 8.0
MIB = 1024 * 1024
MEMBERS = ("expert", "dp", "head")
CHUNK_A = [8, 12, 4, 2]
CHUNK_B = [6, 10, 14, 0]


def layer_norm(values):
    average = jnp.mean(values, axis=-1, keepdims=True)
    centered = values - average
    return centered / jnp.sqrt(jnp.mean(centered * centered, axis=-1, keepdims=True) + epsilon)


def unit_rows(values):
    return values / jnp.sqrt(jnp.mean(values * values, axis=-1, keepdims=True) + epsilon)


def modulate(values, mod_ref):
    return (layer_norm(values.astype(jnp.float32)) * (1.0 + mod_ref[1]) + mod_ref[0]).astype(jnp.bfloat16)


def fetch(pairs, sems):
    copies = [pltpu.make_async_copy(src, dst, sems.at[i]) for i, (src, dst) in enumerate(pairs)]
    for copy in copies:
        copy.start()
    for copy in copies:
        copy.wait()


def own_rows_kernel(own_hbm, mod_hbm, ids_hbm, rows_ref, mod_ref, ids_ref, own, sems):
    fetch([(own_hbm, own), (mod_hbm, mod_ref), (ids_hbm, ids_ref)], sems)
    rows_ref[...] = modulate(own[0], mod_ref)


def own_rows(own, modulation, ids):
    hbm, vmem = pl.BlockSpec(memory_space=pltpu.HBM), pl.BlockSpec(memory_space=pltpu.VMEM)
    return pl.pallas_call(
        own_rows_kernel,
        in_specs=[hbm] * 3,
        out_specs=[vmem] * 3,
        out_shape=[
            jax.ShapeDtypeStruct(own.shape[1:], jnp.bfloat16),
            jax.ShapeDtypeStruct(modulation.shape, modulation.dtype),
            jax.ShapeDtypeStruct(ids.shape, ids.dtype),
        ],
        scratch_shapes=[pltpu.VMEM(own.shape, own.dtype), pltpu.SemaphoreType.DMA((3,))],
        compiler_params=pltpu.CompilerParams(vmem_limit_bytes=16 * MIB),
        cost_estimate=pl.CostEstimate(flops=8 * own.size, bytes_accessed=4 * own.size, transcendentals=0),
        name="own_rows",
    )(own, modulation, ids)


def prep_kernel(
    chips, capacity, me_ref, own_ids, other_ids, own_rows_ref, other, mod, rows_ref, code_ref, *out_refs
):
    tokens = own_rows_ref.shape[0]
    both = 2 * tokens
    rows_ref[:tokens, :] = own_rows_ref[...]
    rows_ref[tokens:, :] = modulate(other[0], mod)
    me = me_ref[0]
    ids = jnp.concatenate([own_ids[0], other_ids[0]], axis=1)
    experts = lax.broadcasted_iota(jnp.int32, (EXPERTS, both), 0)
    named = [experts == ids[j : j + 1, :] for j in range(TOP)]
    tally = functools.reduce(jnp.logical_or, named).astype(jnp.float32).astype(jnp.bfloat16)
    earlier = lax.broadcasted_iota(jnp.int32, (both, both), 0)
    later = lax.broadcasted_iota(jnp.int32, (both, both), 1)
    before = jnp.logical_and(earlier < later, jnp.logical_or(later < tokens, earlier >= tokens))
    rank = jnp.dot(
        tally, before.astype(jnp.float32).astype(jnp.bfloat16), preferred_element_type=jnp.float32
    )
    second = jnp.where(lax.broadcasted_iota(jnp.int32, (1, both), 1) >= tokens, capacity, 0)
    slots = lax.broadcasted_iota(jnp.int32, (2 * chips * capacity, both), 0)
    hit = None
    for j in range(TOP):
        own_rank = jnp.sum(jnp.where(named[j], rank, 0.0), axis=0, keepdims=True).astype(jnp.int32)
        away = jnp.bitwise_xor(ids[j : j + 1, :], me)
        code = lax.shift_right_logical(away, 1) * (2 * capacity) + second + own_rank
        code = jnp.where(jnp.bitwise_and(away, 1) == 0, code, -1)
        code_ref[j : j + 1, :] = code
        hit = slots == code if hit is None else jnp.logical_or(hit, slots == code)
    select = hit.astype(jnp.float32).astype(jnp.bfloat16)
    for p, out_ref in enumerate(out_refs):
        out_ref[...] = jnp.dot(
            select[2 * p * capacity : 2 * (p + 1) * capacity, :],
            rows_ref[...],
            preferred_element_type=jnp.float32,
        ).astype(jnp.bfloat16)


def prep(me, own_ids, other_ids, rows, other, modulation, chips, capacity):
    tokens, width = rows.shape
    vmem = pl.BlockSpec(memory_space=pltpu.VMEM)
    return pl.pallas_call(
        functools.partial(prep_kernel, chips, capacity),
        in_specs=[pl.BlockSpec(memory_space=pltpu.SMEM)] + [vmem] * 5,
        out_specs=[vmem] * (2 + chips),
        out_shape=[
            jax.ShapeDtypeStruct((2 * tokens, width), jnp.bfloat16),
            jax.ShapeDtypeStruct((TOP, 2 * tokens), jnp.int32),
        ]
        + [jax.ShapeDtypeStruct((2 * capacity, width), jnp.bfloat16)] * chips,
        compiler_params=pltpu.CompilerParams(vmem_limit_bytes=16 * MIB),
        cost_estimate=pl.CostEstimate(
            flops=8 * chips * capacity * tokens * width,
            bytes_accessed=4 * chips * capacity * width,
            transcendentals=0,
        ),
        name="prep",
    )(me, own_ids, other_ids, rows, other, modulation)


RESIDENT = 1


def weight_tile(units):
    return 768 if units % 768 == 0 else 128


def resident_kernel(gate_hbm, up_hbm, down_hbm, gate_ref, up_ref, down_ref, sems):
    part = pl.ds(0, gate_ref.shape[1])
    fetch(
        [(gate_hbm.at[:, part], gate_ref), (up_hbm.at[:, part], up_ref), (down_hbm.at[part, :], down_ref)], sems
    )


def resident(gate_weight, up_weight, down_weight):
    width, units = gate_weight.shape
    kept = RESIDENT * weight_tile(units)
    vmem, hbm = pl.BlockSpec(memory_space=pltpu.VMEM), pl.BlockSpec(memory_space=pltpu.HBM)
    return pl.pallas_call(
        resident_kernel,
        in_specs=[hbm] * 3,
        out_specs=[vmem] * 3,
        out_shape=[
            jax.ShapeDtypeStruct((width, kept), jnp.bfloat16),
            jax.ShapeDtypeStruct((width, kept), jnp.bfloat16),
            jax.ShapeDtypeStruct((kept, width), jnp.bfloat16),
        ],
        scratch_shapes=[pltpu.SemaphoreType.DMA((3,))],
        compiler_params=pltpu.CompilerParams(vmem_limit_bytes=46 * MIB),
        cost_estimate=pl.CostEstimate(flops=0, bytes_accessed=6 * width * kept, transcendentals=0),
        name="resident",
    )(gate_weight, up_weight, down_weight)


def ffn_kernel(blocks, tiles, *refs):
    row_refs = refs[:blocks]
    kept_gate, kept_up, kept_down, gate_hbm, up_hbm, down_hbm = refs[blocks : blocks + 6]
    out_refs = refs[blocks + 6 : 2 * blocks + 6]
    rows, total, hidden, gate, up, down, sems = refs[2 * blocks + 6 :]
    size = row_refs[0].shape[0]
    slots, tile = down.shape[0], down.shape[1]

    def copies(step):
        slot, part = lax.rem(step, slots), pl.ds(pl.multiple_of(step * tile, tile), tile)
        return (
            pltpu.make_async_copy(gate_hbm.at[:, part], gate.at[slot], sems.at[0, slot]),
            pltpu.make_async_copy(up_hbm.at[:, part], up.at[slot], sems.at[1, slot]),
            pltpu.make_async_copy(down_hbm.at[part, :], down.at[slot], sems.at[2, slot]),
        )

    def start(step):
        for copy in copies(step):
            copy.start()

    def units_of(gate_tile, up_tile):
        gate_vals = jnp.dot(rows[...], gate_tile, preferred_element_type=jnp.float32)
        up_vals = jnp.dot(rows[...], up_tile, preferred_element_type=jnp.float32)
        return gate_vals, up_vals

    def activate(gate_vals, up_vals):
        return (gate_vals / (1.0 + jnp.exp(-gate_vals)) * up_vals).astype(jnp.bfloat16)

    def part_of(step):
        return slice(step * tile, (step + 1) * tile)

    for step in range(RESIDENT, min(RESIDENT + slots, tiles)):
        start(jnp.int32(step))
    for i in range(blocks):
        rows[i * size : (i + 1) * size, :] = row_refs[i][...]
    hidden[0] = activate(*units_of(kept_gate[:, part_of(0)], kept_up[:, part_of(0)]))

    for step in range(1, RESIDENT):
        vals = units_of(kept_gate[:, part_of(step)], kept_up[:, part_of(step)])
        term = jnp.dot(hidden[(step - 1) % 2], kept_down[part_of(step - 1), :], preferred_element_type=jnp.float32)
        total[...] = term if step == 1 else total[...] + term
        hidden[step % 2] = activate(*vals)

    def wait_units(step):
        gate_copy, up_copy, _ = copies(step)
        gate_copy.wait()
        up_copy.wait()

    wait_units(jnp.int32(RESIDENT))
    vals = units_of(gate[RESIDENT % slots], up[RESIDENT % slots])
    term = jnp.dot(
        hidden[(RESIDENT - 1) % 2], kept_down[part_of(RESIDENT - 1), :], preferred_element_type=jnp.float32
    )
    total[...] = term if RESIDENT == 1 else total[...] + term
    hidden[RESIDENT % 2] = activate(*vals)

    def body(step, carry):
        slot, last = lax.rem(step, slots), lax.rem(step - 1, slots)
        wait_units(step)
        copies(step - 1)[2].wait()
        now = lax.rem(step, 2)
        vals = units_of(gate[slot], up[slot])
        total[...] += jnp.dot(hidden[1 - now], down[last], preferred_element_type=jnp.float32)
        hidden[now] = activate(*vals)

        @pl.when(step + slots - 1 < tiles)
        def _():
            start(step + slots - 1)

        return carry

    lax.fori_loop(RESIDENT + 1, tiles, body, 0)
    copies(jnp.int32(tiles - 1))[2].wait()
    done = total[...] + jnp.dot(
        hidden[(tiles - 1) % 2], down[(tiles - 1) % slots], preferred_element_type=jnp.float32
    )
    for i in range(blocks):
        out_refs[i][...] = done[i * size : (i + 1) * size, :].astype(jnp.bfloat16)


def ffn(row_blocks, kept, gate_weight, up_weight, down_weight):
    blocks = len(row_blocks)
    size, width = row_blocks[0].shape
    units = gate_weight.shape[1]
    tile = weight_tile(units)
    rows, slots = blocks * size, 3
    vmem, hbm = pl.BlockSpec(memory_space=pltpu.VMEM), pl.BlockSpec(memory_space=pltpu.HBM)
    return pl.pallas_call(
        functools.partial(ffn_kernel, blocks, units // tile),
        in_specs=[vmem] * (blocks + 3) + [hbm] * 3,
        out_specs=[vmem] * blocks,
        out_shape=[jax.ShapeDtypeStruct((size, width), jnp.bfloat16)] * blocks,
        scratch_shapes=[
            pltpu.VMEM((rows, width), jnp.bfloat16),
            pltpu.VMEM((rows, width), jnp.float32),
            pltpu.VMEM((2, rows, tile), jnp.bfloat16),
            pltpu.VMEM((slots, width, tile), jnp.bfloat16),
            pltpu.VMEM((slots, width, tile), jnp.bfloat16),
            pltpu.VMEM((slots, tile, width), jnp.bfloat16),
            pltpu.SemaphoreType.DMA((3, slots)),
        ],
        compiler_params=pltpu.CompilerParams(vmem_limit_bytes=36 * MIB),
        cost_estimate=pl.CostEstimate(
            flops=6 * rows * width * units,
            bytes_accessed=6 * width * units,
            transcendentals=rows * units,
        ),
        name="ffn",
    )(*row_blocks, *kept, gate_weight, up_weight, down_weight)


def routes_kernel(rows_ref, router_ref, own_ids_ref, other_ids_ref, code_ref, routes_ref):
    logits = lax.dot_general(
        router_ref[...],
        rows_ref[...].astype(jnp.float32),
        (((1,), (1,)), ((), ())),
        precision=lax.Precision.HIGHEST,
        preferred_element_type=jnp.float32,
    )
    ids = jnp.concatenate([own_ids_ref[0], other_ids_ref[0]], axis=1)
    experts = lax.broadcasted_iota(jnp.int32, logits.shape, 0)
    picked = [
        jnp.sum(jnp.where(experts == ids[j : j + 1, :], logits, 0.0), axis=0, keepdims=True)
        for j in range(TOP)
    ]
    first = 1.0 / (1.0 + jnp.exp(picked[1] - picked[0]))
    line = lax.broadcasted_iota(jnp.int32, (8, first.shape[1]), 0)
    table = jnp.where(line == 0, first, 0.0)
    for j in range(TOP):
        table = jnp.where(line == j + 1, code_ref[j : j + 1, :].astype(jnp.float32), table)
    routes_ref[...] = jnp.transpose(table)


def route_table(rows, router, own_ids, other_ids, code):
    vmem = pl.BlockSpec(memory_space=pltpu.VMEM)
    return pl.pallas_call(
        routes_kernel,
        in_specs=[vmem] * 5,
        out_specs=vmem,
        out_shape=jax.ShapeDtypeStruct((rows.shape[0], 8), jnp.float32),
        compiler_params=pltpu.CompilerParams(vmem_limit_bytes=16 * MIB),
        cost_estimate=pl.CostEstimate(
            flops=12 * rows.size * EXPERTS, bytes_accessed=2 * rows.size, transcendentals=0
        ),
        name="route_table",
    )(rows, router, own_ids, other_ids, code)


def side_kernel(qkv_hbm, q_ref, kv_ref, qkv, sems):
    fetch([(qkv_hbm, qkv)], sems)

    def unit(values):
        return (
            values / jnp.sqrt(jnp.mean(values * values, axis=0, keepdims=True) + epsilon)
        ).astype(jnp.bfloat16)

    for h in range(qkv.shape[0]):
        q_ref[h] = unit(qkv[h, :HD, :].astype(jnp.float32))
        kv_ref[h, :HD, :] = unit(qkv[h, HD : 2 * HD, :].astype(jnp.float32))
        kv_ref[h, HD:, :] = qkv[h, 2 * HD :, :]


def side(qkv):
    heads, _, tokens = qkv.shape
    vmem, hbm = pl.BlockSpec(memory_space=pltpu.VMEM), pl.BlockSpec(memory_space=pltpu.HBM)
    return pl.pallas_call(
        side_kernel,
        in_specs=[hbm],
        out_specs=[vmem] * 2,
        out_shape=[
            jax.ShapeDtypeStruct((heads, HD, tokens), jnp.bfloat16),
            jax.ShapeDtypeStruct((heads, 2 * HD, tokens), jnp.bfloat16),
        ],
        scratch_shapes=[pltpu.VMEM(qkv.shape, qkv.dtype), pltpu.SemaphoreType.DMA((1,))],
        compiler_params=pltpu.CompilerParams(vmem_limit_bytes=16 * MIB),
        cost_estimate=pl.CostEstimate(flops=6 * qkv.size, bytes_accessed=4 * qkv.size, transcendentals=0),
        name="side",
    )(qkv)


def attend_kernel(pieces, head_ref, q_ref, *refs):
    kv_refs = refs[:pieces]
    out_ref, keep_ref, send_ref, mix = refs[pieces:]
    heads, _, queries = q_ref.shape
    for h in range(heads):
        sums, weighted = None, None
        for kv_ref in kv_refs:
            scores = lax.dot_general(
                kv_ref[h, :HD, :], q_ref[h], (((0,), (0,)), ((), ())), preferred_element_type=jnp.float32
            ) * (score_scale / HD)
            weights = jnp.exp(scores - score_scale)
            part = jnp.sum(weights, axis=0, keepdims=True)
            value = jnp.dot(
                kv_ref[h, HD:, :], weights.astype(jnp.bfloat16), preferred_element_type=jnp.float32
            )
            sums = part if sums is None else sums + part
            weighted = value if weighted is None else weighted + value
        attended = (weighted / sums).astype(jnp.bfloat16)
        term = lax.dot_general(
            attended, out_ref[h], (((0,), (0,)), ((), ())), preferred_element_type=jnp.float32
        )
        if h == 0:
            mix[...] = term
        else:
            mix[...] += term
    half = queries // 2
    mine = head_ref[0]
    keep_ref[...] = mix[pl.ds(pl.multiple_of(mine * half, half), half), :]
    send_ref[...] = mix[pl.ds(pl.multiple_of((1 - mine) * half, half), half), :].astype(jnp.bfloat16)


def attend(head, queries, kv_pieces, guide_out):
    heads, _, count = queries.shape
    keys = sum(piece.shape[2] for piece in kv_pieces)
    wide = guide_out.shape[-1]
    vmem = pl.BlockSpec(memory_space=pltpu.VMEM)
    return pl.pallas_call(
        functools.partial(attend_kernel, len(kv_pieces)),
        in_specs=[pl.BlockSpec(memory_space=pltpu.SMEM)] + [vmem] * (2 + len(kv_pieces)),
        out_specs=[vmem, vmem],
        out_shape=[
            jax.ShapeDtypeStruct((count // 2, wide), jnp.float32),
            jax.ShapeDtypeStruct((count // 2, wide), jnp.bfloat16),
        ],
        scratch_shapes=[pltpu.VMEM((count, wide), jnp.float32)],
        compiler_params=pltpu.CompilerParams(vmem_limit_bytes=16 * MIB),
        cost_estimate=pl.CostEstimate(
            flops=4 * heads * count * keys * HD,
            bytes_accessed=4 * heads * keys * HD,
            transcendentals=heads * count * keys,
        ),
        name="attend",
    )(head, queries, *kv_pieces, guide_out)


def combine_kernel(chips, routes_ref, *refs):
    blocks = len(chips)
    row_refs, refs = refs[:blocks], refs[blocks:]
    before_refs, (keep_ref, send_ref, rows, sems) = refs[:-4], refs[-4:]
    size = row_refs[0].shape[0]
    if before_refs:
        for i in range(blocks):
            rows[i * size : (i + 1) * size, :] = row_refs[i][...]
    else:
        fetch([(row_refs[i], rows.at[pl.ds(i * size, size), :]) for i in range(blocks)], sems)
    tokens = routes_ref.shape[0] // 2
    lane = lax.broadcasted_iota(jnp.int32, (tokens, blocks * size), 1)
    slots = lane
    for i, chip in enumerate(chips):
        inside = jnp.logical_and(lane >= i * size, lane < (i + 1) * size)
        slots = jnp.where(inside, lane + (chip - i) * size, slots)
    slots = slots.astype(jnp.float32)
    for i, out_ref in enumerate((keep_ref, send_ref)):
        part = slice(i * tokens, (i + 1) * tokens)
        first = routes_ref[part, 0:1]
        total = before_refs[i][...] if before_refs else None
        for j, weight in enumerate((first, 1.0 - first)):
            pick = (slots == routes_ref[part, j + 1 : j + 2]).astype(jnp.float32).astype(jnp.bfloat16)
            term = weight * jnp.dot(pick, rows[...], preferred_element_type=jnp.float32)
            total = term if total is None else total + term
        out_ref[...] = total.astype(out_ref.dtype)


def combine(row_blocks, chips, routes, before, send_type):
    blocks = len(row_blocks)
    size, width = row_blocks[0].shape
    tokens = routes.shape[0] // 2
    vmem = pl.BlockSpec(memory_space=pltpu.VMEM)
    return pl.pallas_call(
        functools.partial(combine_kernel, chips),
        in_specs=[vmem] + [vmem if before else pl.BlockSpec(memory_space=pl.ANY)] * blocks + [vmem] * len(before),
        out_specs=[vmem] * 2,
        out_shape=[
            jax.ShapeDtypeStruct((tokens, width), jnp.float32),
            jax.ShapeDtypeStruct((tokens, width), send_type),
        ],
        scratch_shapes=[
            pltpu.VMEM((blocks * size, width), jnp.bfloat16),
            pltpu.SemaphoreType.DMA((blocks,)),
        ],
        compiler_params=pltpu.CompilerParams(vmem_limit_bytes=16 * MIB),
        cost_estimate=pl.CostEstimate(
            flops=8 * tokens * blocks * size * width,
            bytes_accessed=2 * blocks * size * width,
            transcendentals=0,
        ),
        name="combine",
    )(routes, *row_blocks, *before)


def finish_kernel(
    keep_moe_ref, got_moe_ref, hidden_ref, mod_ref, final_ref, keep_ref, got_ref, guide_final_ref, latent_ref,
    guidance_ref, step_ref, out_ref
):
    def velocity(weight_ref, values):
        return lax.dot_general(
            weight_ref[...],
            layer_norm(values).astype(jnp.bfloat16),
            (((1,), (1,)), ((), ())),
            preferred_element_type=jnp.float32,
        )

    moe_out = keep_moe_ref[...] + got_moe_ref[...].astype(jnp.float32)
    main_velocity = velocity(final_ref, hidden_ref[0].astype(jnp.float32) + mod_ref[2] * moe_out)
    guide_velocity = velocity(guide_final_ref, keep_ref[...] + got_ref[...].astype(jnp.float32))
    guided = guide_velocity + guidance_ref[0] * (main_velocity - guide_velocity)
    out_ref[0] = latent_ref[0] + step_ref[0] * guided


def finish(keep_moe, got_moe, hidden, modulation, main_final, keep, got, guide_final, latent, guidance, step_size):
    vmem = pl.BlockSpec(memory_space=pltpu.VMEM)
    smem = pl.BlockSpec(memory_space=pltpu.SMEM)
    return pl.pallas_call(
        finish_kernel,
        in_specs=[vmem] * 9 + [smem] * 2,
        out_specs=vmem,
        out_shape=jax.ShapeDtypeStruct(latent.shape, latent.dtype),
        compiler_params=pltpu.CompilerParams(vmem_limit_bytes=16 * MIB),
        cost_estimate=pl.CostEstimate(flops=hidden.size * 64, bytes_accessed=hidden.size * 8, transcendentals=0),
        name="finish",
    )(keep_moe, got_moe, hidden, modulation, main_final, keep, got, guide_final, latent, guidance, step_size)


def direct_body(*args):
    return direct_step(*args)


def direct_step(
    hidden, modulation, router_weight, route_ids, gate_weight, up_weight, down_weight, main_final, guide_qkv,
    guide_out, guide_final, latent, guidance, step_size,
):
    tokens = hidden.shape[1]
    devices = lax.axis_size(MEMBERS)
    capacity = max(2, 2 * tokens * TOP // EXPERTS)
    me = lax.axis_index(MEMBERS).astype(jnp.int32)[None]
    head = lax.axis_index("head").astype(jnp.int32)[None]

    def swap(block, k):
        if k == 0:
            return block
        return lax.ppermute(block, MEMBERS, [(i, i ^ k) for i in range(devices)])

    modulation = jnp.transpose(modulation, (1, 0, 2))
    ids = jnp.transpose(route_ids, (0, 2, 1))
    other = swap(hidden, 1)
    other_ids = swap(ids, 1)
    rows, near_modulation, near_ids = own_rows(hidden, modulation, ids)
    rows, code, *outgoing = prep(
        me, near_ids, other_ids, rows, other, near_modulation, devices // 2, capacity
    )
    rows_a = [swap(outgoing[k // 2], k) for k in CHUNK_A]
    rows_b = [swap(outgoing[k // 2], k) for k in CHUNK_B]
    queries, kv = side(jnp.transpose(guide_qkv[0], (1, 2, 0)))
    weights, _ = lax.optimization_barrier(((gate_weight, up_weight, down_weight), kv))
    kept = resident(*weights)
    far = swap(kv, 8)
    near = swap(kv, 4)
    rows_a, queries = lax.optimization_barrier((rows_a, queries))

    done_a = ffn(rows_a, kept, gate_weight, up_weight, down_weight)
    back_a = [swap(block, k) for block, k in zip(done_a, CHUNK_A)]

    done_b = ffn(rows_b, kept, gate_weight, up_weight, down_weight)
    done_b, queries, back_a, far, near, rows = lax.optimization_barrier(
        (done_b, queries, back_a, far, near, rows)
    )
    back_b = [swap(block, k) for block, k in zip(done_b, CHUNK_B)]
    relayed = swap(far, 4)

    keep, send = attend(head, queries, [kv, near, far, relayed], guide_out)
    got = swap(send, 1)
    routes = route_table(rows, router_weight.T, near_ids, other_ids, code)
    sums = combine(back_a, [k // 2 for k in CHUNK_A], routes, (), jnp.float32)
    keep_moe, send_moe = combine(back_b, [k // 2 for k in CHUNK_B], routes, sums, jnp.bfloat16)
    got_moe = swap(send_moe, 1)
    result = finish(
        keep_moe, got_moe, hidden, modulation, main_final.T, keep, got, guide_final.T,
        jnp.transpose(latent, (0, 2, 1)), guidance, step_size,
    )
    return jnp.transpose(result, (0, 2, 1))


def route_slots(flat_ids, block_slots, per_index, copies):
    route_flat = flat_ids.reshape(-1)
    one_hot = (route_flat[:, None] == jnp.arange(EXPERTS, dtype=jnp.int32)[None, :]).astype(
        jnp.int32
    )
    earlier = jnp.cumsum(one_hot, axis=0) - one_hot
    earlier_count = jnp.sum(earlier * one_hot, axis=1)
    slot_pos = route_flat % per_index * block_slots + earlier_count
    targets = (
        route_flat[:, None] * copies + jnp.arange(copies, dtype=jnp.int32)[None, :]
    ) // per_index
    return (targets, slot_pos)


def expert_hidden(
    rows, positions, gate_weight, up_weight, my_expert, index_first, block_slots, copies
):
    owner_expert = (index_first + positions // block_slots) // copies
    keep_mask = (owner_expert == my_expert).astype(jnp.float32)[:, None]
    gate_vals = jnp.dot(rows, gate_weight, preferred_element_type=jnp.float32)
    up_vals = jnp.dot(rows, up_weight, preferred_element_type=jnp.float32)
    return (jax.nn.silu(gate_vals) * up_vals * keep_mask).astype(jnp.bfloat16)


def spread_body(
    hidden,
    modulation,
    router_weight,
    route_ids,
    gate_weight,
    up_weight,
    down_weight,
    main_final,
    guide_qkv,
    guide_out,
    guide_final,
    latent,
    guidance,
    step_size,
):
    lat_dev, tok_dev, width = hidden.shape
    experts_axis = lax.axis_size("expert")
    group_size = lax.axis_size(("dp", "head"))
    slice_units = gate_weight.shape[1]
    index_units = slice_units * group_size
    if EXPERTS >= experts_axis:
        per_index = EXPERTS // experts_axis
        copies = 1
    else:
        per_index = 1
        copies = experts_axis // EXPERTS
    capacity = max(2, 2 * tok_dev * TOP // EXPERTS)
    block_slots = lat_dev * capacity
    slot_count = per_index * block_slots
    my_index = lax.axis_index("expert")
    my_member = lax.axis_index(("dp", "head"))
    my_expert = (my_index * index_units + my_member * slice_units) // FF
    index_first = my_index * per_index
    hidden_float = hidden.astype(jnp.float32)
    modulated = (
        layer_norm(hidden_float) * (1.0 + modulation[:, 1][:, None, :])
        + modulation[:, 0][:, None, :]
    ).astype(jnp.bfloat16)
    row_count = lat_dev * tok_dev
    flat_rows = modulated.reshape(row_count, width)
    logits = jnp.dot(flat_rows.astype(jnp.float32), router_weight, precision=lax.Precision.HIGHEST)
    flat_ids = route_ids.reshape(row_count, TOP)
    picked = jnp.take_along_axis(logits, flat_ids, axis=1)
    first_weight = jax.nn.sigmoid(picked[:, 0] - picked[:, 1])
    route_weight = jnp.stack([first_weight, 1.0 - first_weight], axis=1)
    route_count = row_count * TOP
    route_token = jnp.arange(route_count, dtype=jnp.int32) // TOP
    targets, slot_pos = route_slots(flat_ids, block_slots, per_index, copies)
    outgoing = jnp.zeros((experts_axis, slot_count, width), jnp.bfloat16)
    payload = jnp.broadcast_to(flat_rows[route_token][:, None, :], (route_count, copies, width))
    outgoing = outgoing.at[targets, slot_pos[:, None]].set(payload)
    received = lax.all_to_all(outgoing, "expert", split_axis=0, concat_axis=0, tiled=True)
    received_rows = received.reshape(experts_axis * slot_count, width)
    piece = lax.all_gather(received_rows, ("dp", "head"), axis=0, tiled=True)
    positions = jnp.arange(piece.shape[0], dtype=jnp.int32) % slot_count
    activated = expert_hidden(
        piece, positions, gate_weight, up_weight, my_expert, index_first, block_slots, copies
    )
    term = jnp.dot(activated, down_weight, preferred_element_type=jnp.float32)
    row_sums = lax.psum_scatter(
        lax.optimization_barrier(term.astype(jnp.bfloat16))
        .astype(jnp.float32)
        .astype(jnp.bfloat16),
        ("dp", "head"),
        scatter_dimension=0,
        tiled=True,
    ).astype(jnp.float32)
    returned = lax.all_to_all(
        row_sums.reshape(experts_axis, slot_count, width).astype(jnp.bfloat16),
        "expert",
        split_axis=0,
        concat_axis=0,
        tiled=True,
    ).astype(jnp.float32)
    gathered_back = returned[targets, slot_pos[:, None]]
    per_route = jnp.sum(gathered_back, axis=1).reshape(row_count, TOP, width)
    moe_out = jnp.sum(per_route * route_weight[:, :, None], axis=1)
    updated = hidden_float + modulation[:, 2][:, None, :] * moe_out.reshape(lat_dev, tok_dev, width)
    main_norm = layer_norm(updated).astype(jnp.bfloat16)
    main_velocity = jnp.dot(
        main_norm.reshape(row_count, width), main_final, preferred_element_type=jnp.float32
    ).reshape(lat_dev, tok_dev, P_SIZE)
    queries = unit_rows(guide_qkv[..., :HD].astype(jnp.float32)).astype(jnp.bfloat16)
    unit_keys = unit_rows(guide_qkv[..., HD : 2 * HD].astype(jnp.float32)).astype(jnp.bfloat16)
    key_value = jnp.concatenate([unit_keys, guide_qkv[..., 2 * HD :]], axis=-1)
    piece = lax.all_gather(key_value, "expert", axis=1, tiled=True)
    key_piece = piece[..., :HD]
    value_piece = piece[..., HD:]
    scores = jnp.einsum(
        "lqhc,lkhc->lhqk", queries, key_piece, preferred_element_type=jnp.float32
    ) * (score_scale / HD)
    weights = jnp.exp(scores - score_scale)
    weighted_sum = jnp.einsum(
        "lhqk,lkhc->lqhc",
        weights.astype(jnp.bfloat16),
        value_piece,
        preferred_element_type=jnp.float32,
    )
    weight_total = jnp.transpose(jnp.sum(weights, axis=-1), (0, 2, 1))
    attended = (weighted_sum / weight_total[..., None]).astype(jnp.bfloat16)
    partial_mix = jnp.einsum(
        "lqhc,hcd->lqd", attended, guide_out, preferred_element_type=jnp.float32
    )
    guide_mix = lax.psum_scatter(
        partial_mix.astype(jnp.bfloat16), "head", scatter_dimension=1, tiled=True
    ).astype(jnp.float32)
    guide_norm = layer_norm(guide_mix).astype(jnp.bfloat16)
    guide_width = guide_norm.shape[-1]
    guide_velocity = jnp.dot(
        guide_norm.reshape(row_count, guide_width), guide_final, preferred_element_type=jnp.float32
    ).reshape(lat_dev, tok_dev, P_SIZE)
    guided = guide_velocity + guidance[:, None, None] * (main_velocity - guide_velocity)
    return latent + step_size[:, None, None] * guided


def solution(mesh):
    in_specs = (
        P(("groups", "dp"), ("expert", "head"), None),
        P(("groups", "dp"), None, None),
        P(),
        P(("groups", "dp"), ("expert", "head"), None),
        P(None, ("expert", "dp", "head")),
        P(None, ("expert", "dp", "head")),
        P(("expert", "dp", "head"), None),
        P(),
        P(("groups", "dp"), "expert", "head", None),
        P("head", None, None),
        P(),
        P(("groups", "dp"), ("expert", "head"), None),
        P(("groups", "dp")),
        P(("groups", "dp")),
    )
    out_specs = P(("groups", "dp"), ("expert", "head"), None)
    sizes = dict(mesh.shape)
    members = sizes["expert"] * sizes["dp"] * sizes["head"]
    direct = members == EXPERTS and sizes["expert"] == 4 and sizes["head"] == 2
    body = direct_body if direct else spread_body
    return jax.shard_map(body, mesh=mesh, in_specs=in_specs, out_specs=out_specs, check_vma=False)
```

```python
import functools

import jax
import jax.numpy as jnp
from jax import lax
from jax.experimental import pallas as pl
from jax.experimental.pallas import tpu as pltpu
from jax.sharding import PartitionSpec as P


FF = 6144
EXPERTS = 16
TOP = 2
HD = 64
P_SIZE = 16


epsilon = 1e-06
score_scale = 8.0
MIB = 1024 * 1024
MEMBERS = ("expert", "dp", "head")
CHUNK_A = [8, 12, 4, 2]
CHUNK_B = [6, 10, 14, 0]
BACK_A = [8, 12, 4]


def layer_norm(values):
    average = jnp.mean(values, axis=-1, keepdims=True)
    centered = values - average
    return centered / jnp.sqrt(jnp.mean(centered * centered, axis=-1, keepdims=True) + epsilon)


def unit_rows(values):
    return values / jnp.sqrt(jnp.mean(values * values, axis=-1, keepdims=True) + epsilon)


def modulate(values, mod_ref):
    return (layer_norm(values.astype(jnp.float32)) * (1.0 + mod_ref[1]) + mod_ref[0]).astype(jnp.bfloat16)


def fetch(pairs, sems):
    copies = [pltpu.make_async_copy(src, dst, sems.at[i]) for i, (src, dst) in enumerate(pairs)]
    for copy in copies:
        copy.start()
    for copy in copies:
        copy.wait()


def own_rows_kernel(own_hbm, mod_hbm, ids_hbm, rows_ref, mod_ref, ids_ref, own, sems):
    fetch([(own_hbm, own), (mod_hbm, mod_ref), (ids_hbm, ids_ref)], sems)
    rows_ref[...] = modulate(own[0], mod_ref)


def own_rows(own, modulation, ids):
    hbm, vmem = pl.BlockSpec(memory_space=pltpu.HBM), pl.BlockSpec(memory_space=pltpu.VMEM)
    return pl.pallas_call(
        own_rows_kernel,
        in_specs=[hbm] * 3,
        out_specs=[vmem] * 3,
        out_shape=[
            jax.ShapeDtypeStruct(own.shape[1:], jnp.bfloat16),
            jax.ShapeDtypeStruct(modulation.shape, modulation.dtype),
            jax.ShapeDtypeStruct(ids.shape, ids.dtype),
        ],
        scratch_shapes=[pltpu.VMEM(own.shape, own.dtype), pltpu.SemaphoreType.DMA((3,))],
        compiler_params=pltpu.CompilerParams(vmem_limit_bytes=16 * MIB),
        cost_estimate=pl.CostEstimate(flops=8 * own.size, bytes_accessed=4 * own.size, transcendentals=0),
        name="own_rows",
    )(own, modulation, ids)


def prep_kernel(
    chips, capacity, me_ref, own_ids, other_ids, own_rows_ref, other, mod, rows_ref, code_ref, *out_refs
):
    tokens = own_rows_ref.shape[0]
    both = 2 * tokens
    rows_ref[:tokens, :] = own_rows_ref[...]
    rows_ref[tokens:, :] = modulate(other[0], mod)
    me = me_ref[0]
    ids = jnp.concatenate([own_ids[0], other_ids[0]], axis=1)
    experts = lax.broadcasted_iota(jnp.int32, (EXPERTS, both), 0)
    named = [experts == ids[j : j + 1, :] for j in range(TOP)]
    tally = functools.reduce(jnp.logical_or, named).astype(jnp.float32).astype(jnp.bfloat16)
    earlier = lax.broadcasted_iota(jnp.int32, (both, both), 0)
    later = lax.broadcasted_iota(jnp.int32, (both, both), 1)
    before = jnp.logical_and(earlier < later, jnp.logical_or(later < tokens, earlier >= tokens))
    rank = jnp.dot(
        tally, before.astype(jnp.float32).astype(jnp.bfloat16), preferred_element_type=jnp.float32
    )
    second = jnp.where(lax.broadcasted_iota(jnp.int32, (1, both), 1) >= tokens, capacity, 0)
    slots = lax.broadcasted_iota(jnp.int32, (2 * chips * capacity, both), 0)
    hit = None
    for j in range(TOP):
        own_rank = jnp.sum(jnp.where(named[j], rank, 0.0), axis=0, keepdims=True).astype(jnp.int32)
        away = jnp.bitwise_xor(ids[j : j + 1, :], me)
        code = lax.shift_right_logical(away, 1) * (2 * capacity) + second + own_rank
        code = jnp.where(jnp.bitwise_and(away, 1) == 0, code, -1)
        code_ref[j : j + 1, :] = code
        hit = slots == code if hit is None else jnp.logical_or(hit, slots == code)
    select = hit.astype(jnp.float32).astype(jnp.bfloat16)
    for p, out_ref in enumerate(out_refs):
        out_ref[...] = jnp.dot(
            select[2 * p * capacity : 2 * (p + 1) * capacity, :],
            rows_ref[...],
            preferred_element_type=jnp.float32,
        ).astype(jnp.bfloat16)


def prep(me, own_ids, other_ids, rows, other, modulation, chips, capacity):
    tokens, width = rows.shape
    vmem = pl.BlockSpec(memory_space=pltpu.VMEM)
    return pl.pallas_call(
        functools.partial(prep_kernel, chips, capacity),
        in_specs=[pl.BlockSpec(memory_space=pltpu.SMEM)] + [vmem] * 5,
        out_specs=[vmem] * (2 + chips),
        out_shape=[
            jax.ShapeDtypeStruct((2 * tokens, width), jnp.bfloat16),
            jax.ShapeDtypeStruct((TOP, 2 * tokens), jnp.int32),
        ]
        + [jax.ShapeDtypeStruct((2 * capacity, width), jnp.bfloat16)] * chips,
        compiler_params=pltpu.CompilerParams(vmem_limit_bytes=16 * MIB),
        cost_estimate=pl.CostEstimate(
            flops=8 * chips * capacity * tokens * width,
            bytes_accessed=4 * chips * capacity * width,
            transcendentals=0,
        ),
        name="prep",
    )(me, own_ids, other_ids, rows, other, modulation)


RESIDENT = 1


def weight_tile(units):
    return 768 if units % 768 == 0 else 128


def resident_kernel(gate_hbm, up_hbm, down_hbm, gate_ref, up_ref, down_ref, sems):
    part = pl.ds(0, gate_ref.shape[1])
    fetch(
        [(gate_hbm.at[:, part], gate_ref), (up_hbm.at[:, part], up_ref), (down_hbm.at[part, :], down_ref)], sems
    )


def resident(gate_weight, up_weight, down_weight):
    width, units = gate_weight.shape
    kept = RESIDENT * weight_tile(units)
    vmem, hbm = pl.BlockSpec(memory_space=pltpu.VMEM), pl.BlockSpec(memory_space=pltpu.HBM)
    return pl.pallas_call(
        resident_kernel,
        in_specs=[hbm] * 3,
        out_specs=[vmem] * 3,
        out_shape=[
            jax.ShapeDtypeStruct((width, kept), jnp.bfloat16),
            jax.ShapeDtypeStruct((width, kept), jnp.bfloat16),
            jax.ShapeDtypeStruct((kept, width), jnp.bfloat16),
        ],
        scratch_shapes=[pltpu.SemaphoreType.DMA((3,))],
        compiler_params=pltpu.CompilerParams(vmem_limit_bytes=46 * MIB),
        cost_estimate=pl.CostEstimate(flops=0, bytes_accessed=6 * width * kept, transcendentals=0),
        name="resident",
    )(gate_weight, up_weight, down_weight)


def ffn_kernel(blocks, tiles, *refs):
    row_refs = refs[:blocks]
    kept_gate, kept_up, kept_down, gate_hbm, up_hbm, down_hbm = refs[blocks : blocks + 6]
    out_refs = refs[blocks + 6 : 2 * blocks + 6]
    rows, total, hidden, gate, up, down, sems = refs[2 * blocks + 6 :]
    size = row_refs[0].shape[0]
    slots, tile = down.shape[0], down.shape[1]

    def copies(step):
        slot, part = lax.rem(step, slots), pl.ds(pl.multiple_of(step * tile, tile), tile)
        return (
            pltpu.make_async_copy(gate_hbm.at[:, part], gate.at[slot], sems.at[0, slot]),
            pltpu.make_async_copy(up_hbm.at[:, part], up.at[slot], sems.at[1, slot]),
            pltpu.make_async_copy(down_hbm.at[part, :], down.at[slot], sems.at[2, slot]),
        )

    def start(step):
        for copy in copies(step):
            copy.start()

    def units_of(gate_tile, up_tile):
        gate_vals = jnp.dot(rows[...], gate_tile, preferred_element_type=jnp.float32)
        up_vals = jnp.dot(rows[...], up_tile, preferred_element_type=jnp.float32)
        return gate_vals, up_vals

    def activate(gate_vals, up_vals):
        return (gate_vals / (1.0 + jnp.exp(-gate_vals)) * up_vals).astype(jnp.bfloat16)

    def part_of(step):
        return slice(step * tile, (step + 1) * tile)

    for step in range(RESIDENT, min(RESIDENT + slots, tiles)):
        start(jnp.int32(step))
    for i in range(blocks):
        rows[i * size : (i + 1) * size, :] = row_refs[i][...]
    hidden[0] = activate(*units_of(kept_gate[:, part_of(0)], kept_up[:, part_of(0)]))

    for step in range(1, RESIDENT):
        vals = units_of(kept_gate[:, part_of(step)], kept_up[:, part_of(step)])
        term = jnp.dot(hidden[(step - 1) % 2], kept_down[part_of(step - 1), :], preferred_element_type=jnp.float32)
        total[...] = term if step == 1 else total[...] + term
        hidden[step % 2] = activate(*vals)

    def wait_units(step):
        gate_copy, up_copy, _ = copies(step)
        gate_copy.wait()
        up_copy.wait()

    wait_units(jnp.int32(RESIDENT))
    vals = units_of(gate[RESIDENT % slots], up[RESIDENT % slots])
    term = jnp.dot(
        hidden[(RESIDENT - 1) % 2], kept_down[part_of(RESIDENT - 1), :], preferred_element_type=jnp.float32
    )
    total[...] = term if RESIDENT == 1 else total[...] + term
    hidden[RESIDENT % 2] = activate(*vals)

    def body(step, carry):
        slot, last = lax.rem(step, slots), lax.rem(step - 1, slots)
        wait_units(step)
        copies(step - 1)[2].wait()
        now = lax.rem(step, 2)
        vals = units_of(gate[slot], up[slot])
        total[...] += jnp.dot(hidden[1 - now], down[last], preferred_element_type=jnp.float32)
        hidden[now] = activate(*vals)

        @pl.when(step + slots - 1 < tiles)
        def _():
            start(step + slots - 1)

        return carry

    lax.fori_loop(RESIDENT + 1, tiles, body, 0)
    copies(jnp.int32(tiles - 1))[2].wait()
    done = total[...] + jnp.dot(
        hidden[(tiles - 1) % 2], down[(tiles - 1) % slots], preferred_element_type=jnp.float32
    )
    for i in range(blocks):
        out_refs[i][...] = done[i * size : (i + 1) * size, :].astype(jnp.bfloat16)


def ffn(row_blocks, kept, gate_weight, up_weight, down_weight):
    blocks = len(row_blocks)
    size, width = row_blocks[0].shape
    units = gate_weight.shape[1]
    tile = weight_tile(units)
    rows, slots = blocks * size, 3
    vmem, hbm = pl.BlockSpec(memory_space=pltpu.VMEM), pl.BlockSpec(memory_space=pltpu.HBM)
    return pl.pallas_call(
        functools.partial(ffn_kernel, blocks, units // tile),
        in_specs=[vmem] * (blocks + 3) + [hbm] * 3,
        out_specs=[vmem] * blocks,
        out_shape=[jax.ShapeDtypeStruct((size, width), jnp.bfloat16)] * blocks,
        scratch_shapes=[
            pltpu.VMEM((rows, width), jnp.bfloat16),
            pltpu.VMEM((rows, width), jnp.float32),
            pltpu.VMEM((2, rows, tile), jnp.bfloat16),
            pltpu.VMEM((slots, width, tile), jnp.bfloat16),
            pltpu.VMEM((slots, width, tile), jnp.bfloat16),
            pltpu.VMEM((slots, tile, width), jnp.bfloat16),
            pltpu.SemaphoreType.DMA((3, slots)),
        ],
        compiler_params=pltpu.CompilerParams(vmem_limit_bytes=36 * MIB),
        cost_estimate=pl.CostEstimate(
            flops=6 * rows * width * units,
            bytes_accessed=6 * width * units,
            transcendentals=rows * units,
        ),
        name="ffn",
    )(*row_blocks, *kept, gate_weight, up_weight, down_weight)


def routes_kernel(rows_ref, router_ref, own_ids_ref, other_ids_ref, code_ref, routes_ref):
    logits = lax.dot_general(
        router_ref[...],
        rows_ref[...].astype(jnp.float32),
        (((1,), (1,)), ((), ())),
        precision=lax.Precision.HIGHEST,
        preferred_element_type=jnp.float32,
    )
    ids = jnp.concatenate([own_ids_ref[0], other_ids_ref[0]], axis=1)
    experts = lax.broadcasted_iota(jnp.int32, logits.shape, 0)
    picked = [
        jnp.sum(jnp.where(experts == ids[j : j + 1, :], logits, 0.0), axis=0, keepdims=True)
        for j in range(TOP)
    ]
    first = 1.0 / (1.0 + jnp.exp(picked[1] - picked[0]))
    line = lax.broadcasted_iota(jnp.int32, (8, first.shape[1]), 0)
    table = jnp.where(line == 0, first, 0.0)
    for j in range(TOP):
        table = jnp.where(line == j + 1, code_ref[j : j + 1, :].astype(jnp.float32), table)
    routes_ref[...] = jnp.transpose(table)


def route_table(rows, router, own_ids, other_ids, code):
    vmem = pl.BlockSpec(memory_space=pltpu.VMEM)
    return pl.pallas_call(
        routes_kernel,
        in_specs=[vmem] * 5,
        out_specs=vmem,
        out_shape=jax.ShapeDtypeStruct((rows.shape[0], 8), jnp.float32),
        compiler_params=pltpu.CompilerParams(vmem_limit_bytes=16 * MIB),
        cost_estimate=pl.CostEstimate(
            flops=12 * rows.size * EXPERTS, bytes_accessed=2 * rows.size, transcendentals=0
        ),
        name="route_table",
    )(rows, router, own_ids, other_ids, code)


def side_kernel(qkv_hbm, q_ref, kv_ref, qkv, sems):
    fetch([(qkv_hbm, qkv)], sems)

    def unit(values):
        return (
            values / jnp.sqrt(jnp.mean(values * values, axis=0, keepdims=True) + epsilon)
        ).astype(jnp.bfloat16)

    for h in range(qkv.shape[0]):
        q_ref[h] = unit(qkv[h, :HD, :].astype(jnp.float32))
        kv_ref[h, :HD, :] = unit(qkv[h, HD : 2 * HD, :].astype(jnp.float32))
        kv_ref[h, HD:, :] = qkv[h, 2 * HD :, :]


def side(qkv):
    heads, _, tokens = qkv.shape
    vmem, hbm = pl.BlockSpec(memory_space=pltpu.VMEM), pl.BlockSpec(memory_space=pltpu.HBM)
    return pl.pallas_call(
        side_kernel,
        in_specs=[hbm],
        out_specs=[vmem] * 2,
        out_shape=[
            jax.ShapeDtypeStruct((heads, HD, tokens), jnp.bfloat16),
            jax.ShapeDtypeStruct((heads, 2 * HD, tokens), jnp.bfloat16),
        ],
        scratch_shapes=[pltpu.VMEM(qkv.shape, qkv.dtype), pltpu.SemaphoreType.DMA((1,))],
        compiler_params=pltpu.CompilerParams(vmem_limit_bytes=16 * MIB),
        cost_estimate=pl.CostEstimate(flops=6 * qkv.size, bytes_accessed=4 * qkv.size, transcendentals=0),
        name="side",
    )(qkv)


def attend_kernel(pieces, head_ref, q_ref, *refs):
    kv_refs = refs[:pieces]
    out_ref, keep_ref, send_ref, mix = refs[pieces:]
    heads, _, queries = q_ref.shape
    for h in range(heads):
        sums, weighted = None, None
        for kv_ref in kv_refs:
            scores = lax.dot_general(
                kv_ref[h, :HD, :], q_ref[h], (((0,), (0,)), ((), ())), preferred_element_type=jnp.float32
            ) * (score_scale / HD)
            weights = jnp.exp(scores - score_scale)
            part = jnp.sum(weights, axis=0, keepdims=True)
            value = jnp.dot(
                kv_ref[h, HD:, :], weights.astype(jnp.bfloat16), preferred_element_type=jnp.float32
            )
            sums = part if sums is None else sums + part
            weighted = value if weighted is None else weighted + value
        attended = (weighted / sums).astype(jnp.bfloat16)
        term = lax.dot_general(
            attended, out_ref[h], (((0,), (0,)), ((), ())), preferred_element_type=jnp.float32
        )
        if h == 0:
            mix[...] = term
        else:
            mix[...] += term
    half = queries // 2
    mine = head_ref[0]
    keep_ref[...] = mix[pl.ds(pl.multiple_of(mine * half, half), half), :]
    send_ref[...] = mix[pl.ds(pl.multiple_of((1 - mine) * half, half), half), :].astype(jnp.bfloat16)


def attend(head, queries, kv_pieces, guide_out):
    heads, _, count = queries.shape
    keys = sum(piece.shape[2] for piece in kv_pieces)
    wide = guide_out.shape[-1]
    vmem = pl.BlockSpec(memory_space=pltpu.VMEM)
    return pl.pallas_call(
        functools.partial(attend_kernel, len(kv_pieces)),
        in_specs=[pl.BlockSpec(memory_space=pltpu.SMEM)] + [vmem] * (2 + len(kv_pieces)),
        out_specs=[vmem, vmem],
        out_shape=[
            jax.ShapeDtypeStruct((count // 2, wide), jnp.float32),
            jax.ShapeDtypeStruct((count // 2, wide), jnp.bfloat16),
        ],
        scratch_shapes=[pltpu.VMEM((count, wide), jnp.float32)],
        compiler_params=pltpu.CompilerParams(vmem_limit_bytes=16 * MIB),
        cost_estimate=pl.CostEstimate(
            flops=4 * heads * count * keys * HD,
            bytes_accessed=4 * heads * keys * HD,
            transcendentals=heads * count * keys,
        ),
        name="attend",
    )(head, queries, *kv_pieces, guide_out)


def combine_kernel(chips, routes_ref, *refs):
    blocks = len(chips)
    row_refs, refs = refs[:blocks], refs[blocks:]
    before_refs, (keep_ref, send_ref, rows, sems) = refs[:-4], refs[-4:]
    size = row_refs[0].shape[0]
    if before_refs:
        for i in range(blocks):
            rows[i * size : (i + 1) * size, :] = row_refs[i][...]
    else:
        fetch([(row_refs[i], rows.at[pl.ds(i * size, size), :]) for i in range(blocks)], sems)
    tokens = routes_ref.shape[0] // 2
    lane = lax.broadcasted_iota(jnp.int32, (tokens, blocks * size), 1)
    slots = lane
    for i, chip in enumerate(chips):
        inside = jnp.logical_and(lane >= i * size, lane < (i + 1) * size)
        slots = jnp.where(inside, lane + (chip - i) * size, slots)
    slots = slots.astype(jnp.float32)
    for i, out_ref in enumerate((keep_ref, send_ref)):
        part = slice(i * tokens, (i + 1) * tokens)
        first = routes_ref[part, 0:1]
        total = before_refs[i][...] if before_refs else None
        for j, weight in enumerate((first, 1.0 - first)):
            pick = (slots == routes_ref[part, j + 1 : j + 2]).astype(jnp.float32).astype(jnp.bfloat16)
            term = weight * jnp.dot(pick, rows[...], preferred_element_type=jnp.float32)
            total = term if total is None else total + term
        out_ref[...] = total.astype(out_ref.dtype)


def combine(row_blocks, chips, routes, before, send_type):
    blocks = len(row_blocks)
    size, width = row_blocks[0].shape
    tokens = routes.shape[0] // 2
    vmem = pl.BlockSpec(memory_space=pltpu.VMEM)
    return pl.pallas_call(
        functools.partial(combine_kernel, chips),
        in_specs=[vmem] + [vmem if before else pl.BlockSpec(memory_space=pl.ANY)] * blocks + [vmem] * len(before),
        out_specs=[vmem] * 2,
        out_shape=[
            jax.ShapeDtypeStruct((tokens, width), jnp.float32),
            jax.ShapeDtypeStruct((tokens, width), send_type),
        ],
        scratch_shapes=[
            pltpu.VMEM((blocks * size, width), jnp.bfloat16),
            pltpu.SemaphoreType.DMA((blocks,)),
        ],
        compiler_params=pltpu.CompilerParams(vmem_limit_bytes=16 * MIB),
        cost_estimate=pl.CostEstimate(
            flops=8 * tokens * blocks * size * width,
            bytes_accessed=2 * blocks * size * width,
            transcendentals=0,
        ),
        name="combine",
    )(routes, *row_blocks, *before)


def finish_kernel(
    keep_moe_ref, got_moe_ref, hidden_ref, mod_ref, final_ref, keep_ref, got_ref, guide_final_ref, latent_ref,
    guidance_ref, step_ref, out_ref
):
    def velocity(weight_ref, values):
        return lax.dot_general(
            weight_ref[...],
            layer_norm(values).astype(jnp.bfloat16),
            (((1,), (1,)), ((), ())),
            preferred_element_type=jnp.float32,
        )

    moe_out = keep_moe_ref[...] + got_moe_ref[...].astype(jnp.float32)
    main_velocity = velocity(final_ref, hidden_ref[0].astype(jnp.float32) + mod_ref[2] * moe_out)
    guide_velocity = velocity(guide_final_ref, keep_ref[...] + got_ref[...].astype(jnp.float32))
    guided = guide_velocity + guidance_ref[0] * (main_velocity - guide_velocity)
    out_ref[0] = latent_ref[0] + step_ref[0] * guided


def finish(keep_moe, got_moe, hidden, modulation, main_final, keep, got, guide_final, latent, guidance, step_size):
    vmem = pl.BlockSpec(memory_space=pltpu.VMEM)
    smem = pl.BlockSpec(memory_space=pltpu.SMEM)
    return pl.pallas_call(
        finish_kernel,
        in_specs=[vmem] * 9 + [smem] * 2,
        out_specs=vmem,
        out_shape=jax.ShapeDtypeStruct(latent.shape, latent.dtype),
        compiler_params=pltpu.CompilerParams(vmem_limit_bytes=16 * MIB),
        cost_estimate=pl.CostEstimate(flops=hidden.size * 64, bytes_accessed=hidden.size * 8, transcendentals=0),
        name="finish",
    )(keep_moe, got_moe, hidden, modulation, main_final, keep, got, guide_final, latent, guidance, step_size)


def direct_body(*args):
    return direct_step(*args)


def direct_step(
    hidden, modulation, router_weight, route_ids, gate_weight, up_weight, down_weight, main_final, guide_qkv,
    guide_out, guide_final, latent, guidance, step_size,
):
    tokens = hidden.shape[1]
    devices = lax.axis_size(MEMBERS)
    capacity = max(2, 2 * tokens * TOP // EXPERTS)
    me = lax.axis_index(MEMBERS).astype(jnp.int32)[None]
    head = lax.axis_index("head").astype(jnp.int32)[None]

    def swap(block, k):
        if k == 0:
            return block
        return lax.ppermute(block, MEMBERS, [(i, i ^ k) for i in range(devices)])

    modulation = jnp.transpose(modulation, (1, 0, 2))
    ids = jnp.transpose(route_ids, (0, 2, 1))
    other = swap(hidden, 1)
    other_ids = swap(ids, 1)
    rows, near_modulation, near_ids = own_rows(hidden, modulation, ids)
    rows, code, *outgoing = prep(
        me, near_ids, other_ids, rows, other, near_modulation, devices // 2, capacity
    )
    rows_a = [swap(outgoing[k // 2], k) for k in CHUNK_A]
    rows_b = [swap(outgoing[k // 2], k) for k in CHUNK_B]
    queries, kv = side(jnp.transpose(guide_qkv[0], (1, 2, 0)))
    weights, _ = lax.optimization_barrier(((gate_weight, up_weight, down_weight), kv))
    kept = resident(*weights)
    far = swap(kv, 8)
    near = swap(kv, 4)
    rows_a, queries = lax.optimization_barrier((rows_a, queries))

    done_a = ffn(rows_a, kept, gate_weight, up_weight, down_weight)

    done_b = ffn(rows_b, kept, gate_weight, up_weight, down_weight)
    back_a = [swap(block, k) if k in BACK_A else block for block, k in zip(done_a, CHUNK_A)]
    done_b, queries, back_a, far, near, rows = lax.optimization_barrier(
        (done_b, queries, back_a, far, near, rows)
    )
    back_a = [block if k in BACK_A else swap(block, k) for block, k in zip(back_a, CHUNK_A)]
    back_b = [swap(block, k) for block, k in zip(done_b, CHUNK_B)]
    relayed = swap(far, 4)

    keep, send = attend(head, queries, [kv, near, far, relayed], guide_out)
    got = swap(send, 1)
    routes = route_table(rows, router_weight.T, near_ids, other_ids, code)
    back = dict(zip(CHUNK_A + CHUNK_B, back_a + back_b))
    late = [k for k in CHUNK_A + CHUNK_B if k not in BACK_A]
    sums = combine([back[k] for k in BACK_A], [k // 2 for k in BACK_A], routes, (), jnp.float32)
    keep_moe, send_moe = combine(
        [back[k] for k in late], [k // 2 for k in late], routes, sums, jnp.bfloat16
    )
    got_moe = swap(send_moe, 1)
    result = finish(
        keep_moe, got_moe, hidden, modulation, main_final.T, keep, got, guide_final.T,
        jnp.transpose(latent, (0, 2, 1)), guidance, step_size,
    )
    return jnp.transpose(result, (0, 2, 1))


def route_slots(flat_ids, block_slots, per_index, copies):
    route_flat = flat_ids.reshape(-1)
    one_hot = (route_flat[:, None] == jnp.arange(EXPERTS, dtype=jnp.int32)[None, :]).astype(
        jnp.int32
    )
    earlier = jnp.cumsum(one_hot, axis=0) - one_hot
    earlier_count = jnp.sum(earlier * one_hot, axis=1)
    slot_pos = route_flat % per_index * block_slots + earlier_count
    targets = (
        route_flat[:, None] * copies + jnp.arange(copies, dtype=jnp.int32)[None, :]
    ) // per_index
    return (targets, slot_pos)


def expert_hidden(
    rows, positions, gate_weight, up_weight, my_expert, index_first, block_slots, copies
):
    owner_expert = (index_first + positions // block_slots) // copies
    keep_mask = (owner_expert == my_expert).astype(jnp.float32)[:, None]
    gate_vals = jnp.dot(rows, gate_weight, preferred_element_type=jnp.float32)
    up_vals = jnp.dot(rows, up_weight, preferred_element_type=jnp.float32)
    return (jax.nn.silu(gate_vals) * up_vals * keep_mask).astype(jnp.bfloat16)


def spread_body(
    hidden,
    modulation,
    router_weight,
    route_ids,
    gate_weight,
    up_weight,
    down_weight,
    main_final,
    guide_qkv,
    guide_out,
    guide_final,
    latent,
    guidance,
    step_size,
):
    lat_dev, tok_dev, width = hidden.shape
    experts_axis = lax.axis_size("expert")
    group_size = lax.axis_size(("dp", "head"))
    slice_units = gate_weight.shape[1]
    index_units = slice_units * group_size
    if EXPERTS >= experts_axis:
        per_index = EXPERTS // experts_axis
        copies = 1
    else:
        per_index = 1
        copies = experts_axis // EXPERTS
    capacity = max(2, 2 * tok_dev * TOP // EXPERTS)
    block_slots = lat_dev * capacity
    slot_count = per_index * block_slots
    my_index = lax.axis_index("expert")
    my_member = lax.axis_index(("dp", "head"))
    my_expert = (my_index * index_units + my_member * slice_units) // FF
    index_first = my_index * per_index
    hidden_float = hidden.astype(jnp.float32)
    modulated = (
        layer_norm(hidden_float) * (1.0 + modulation[:, 1][:, None, :])
        + modulation[:, 0][:, None, :]
    ).astype(jnp.bfloat16)
    row_count = lat_dev * tok_dev
    flat_rows = modulated.reshape(row_count, width)
    logits = jnp.dot(flat_rows.astype(jnp.float32), router_weight, precision=lax.Precision.HIGHEST)
    flat_ids = route_ids.reshape(row_count, TOP)
    picked = jnp.take_along_axis(logits, flat_ids, axis=1)
    first_weight = jax.nn.sigmoid(picked[:, 0] - picked[:, 1])
    route_weight = jnp.stack([first_weight, 1.0 - first_weight], axis=1)
    route_count = row_count * TOP
    route_token = jnp.arange(route_count, dtype=jnp.int32) // TOP
    targets, slot_pos = route_slots(flat_ids, block_slots, per_index, copies)
    outgoing = jnp.zeros((experts_axis, slot_count, width), jnp.bfloat16)
    payload = jnp.broadcast_to(flat_rows[route_token][:, None, :], (route_count, copies, width))
    outgoing = outgoing.at[targets, slot_pos[:, None]].set(payload)
    received = lax.all_to_all(outgoing, "expert", split_axis=0, concat_axis=0, tiled=True)
    received_rows = received.reshape(experts_axis * slot_count, width)
    piece = lax.all_gather(received_rows, ("dp", "head"), axis=0, tiled=True)
    positions = jnp.arange(piece.shape[0], dtype=jnp.int32) % slot_count
    activated = expert_hidden(
        piece, positions, gate_weight, up_weight, my_expert, index_first, block_slots, copies
    )
    term = jnp.dot(activated, down_weight, preferred_element_type=jnp.float32)
    row_sums = lax.psum_scatter(
        lax.optimization_barrier(term.astype(jnp.bfloat16))
        .astype(jnp.float32)
        .astype(jnp.bfloat16),
        ("dp", "head"),
        scatter_dimension=0,
        tiled=True,
    ).astype(jnp.float32)
    returned = lax.all_to_all(
        row_sums.reshape(experts_axis, slot_count, width).astype(jnp.bfloat16),
        "expert",
        split_axis=0,
        concat_axis=0,
        tiled=True,
    ).astype(jnp.float32)
    gathered_back = returned[targets, slot_pos[:, None]]
    per_route = jnp.sum(gathered_back, axis=1).reshape(row_count, TOP, width)
    moe_out = jnp.sum(per_route * route_weight[:, :, None], axis=1)
    updated = hidden_float + modulation[:, 2][:, None, :] * moe_out.reshape(lat_dev, tok_dev, width)
    main_norm = layer_norm(updated).astype(jnp.bfloat16)
    main_velocity = jnp.dot(
        main_norm.reshape(row_count, width), main_final, preferred_element_type=jnp.float32
    ).reshape(lat_dev, tok_dev, P_SIZE)
    queries = unit_rows(guide_qkv[..., :HD].astype(jnp.float32)).astype(jnp.bfloat16)
    unit_keys = unit_rows(guide_qkv[..., HD : 2 * HD].astype(jnp.float32)).astype(jnp.bfloat16)
    key_value = jnp.concatenate([unit_keys, guide_qkv[..., 2 * HD :]], axis=-1)
    piece = lax.all_gather(key_value, "expert", axis=1, tiled=True)
    key_piece = piece[..., :HD]
    value_piece = piece[..., HD:]
    scores = jnp.einsum(
        "lqhc,lkhc->lhqk", queries, key_piece, preferred_element_type=jnp.float32
    ) * (score_scale / HD)
    weights = jnp.exp(scores - score_scale)
    weighted_sum = jnp.einsum(
        "lhqk,lkhc->lqhc",
        weights.astype(jnp.bfloat16),
        value_piece,
        preferred_element_type=jnp.float32,
    )
    weight_total = jnp.transpose(jnp.sum(weights, axis=-1), (0, 2, 1))
    attended = (weighted_sum / weight_total[..., None]).astype(jnp.bfloat16)
    partial_mix = jnp.einsum(
        "lqhc,hcd->lqd", attended, guide_out, preferred_element_type=jnp.float32
    )
    guide_mix = lax.psum_scatter(
        partial_mix.astype(jnp.bfloat16), "head", scatter_dimension=1, tiled=True
    ).astype(jnp.float32)
    guide_norm = layer_norm(guide_mix).astype(jnp.bfloat16)
    guide_width = guide_norm.shape[-1]
    guide_velocity = jnp.dot(
        guide_norm.reshape(row_count, guide_width), guide_final, preferred_element_type=jnp.float32
    ).reshape(lat_dev, tok_dev, P_SIZE)
    guided = guide_velocity + guidance[:, None, None] * (main_velocity - guide_velocity)
    return latent + step_size[:, None, None] * guided


def solution(mesh):
    in_specs = (
        P(("groups", "dp"), ("expert", "head"), None),
        P(("groups", "dp"), None, None),
        P(),
        P(("groups", "dp"), ("expert", "head"), None),
        P(None, ("expert", "dp", "head")),
        P(None, ("expert", "dp", "head")),
        P(("expert", "dp", "head"), None),
        P(),
        P(("groups", "dp"), "expert", "head", None),
        P("head", None, None),
        P(),
        P(("groups", "dp"), ("expert", "head"), None),
        P(("groups", "dp")),
        P(("groups", "dp")),
    )
    out_specs = P(("groups", "dp"), ("expert", "head"), None)
    sizes = dict(mesh.shape)
    members = sizes["expert"] * sizes["dp"] * sizes["head"]
    direct = members == EXPERTS and sizes["expert"] == 4 and sizes["head"] == 2
    body = direct_body if direct else spread_body
    return jax.shard_map(body, mesh=mesh, in_specs=in_specs, out_specs=out_specs, check_vma=False)
```
